128 devices in a mesh: ice: 64 (over y_hi, z, x, core), hyd: 2 (over y_lo).
Axes of the slice: x: 4, y: 4 (y_hi: 2, y_lo: 2; y = y_hi * 2 + y_lo), z: 4, core: 2. Of those that a mesh axis runs over, the one named last changes fastest.
Arguments:
- viscosity: bfloat16 [20, 1024, 6144], P(None, 'ice', 'hyd'), may hold values from 0.29882812 to 3
- driving_stress: float32 [2, 1024, 6144], P(None, 'ice', 'hyd'), may hold values from -120 to 120
- ice_mask: int32 [1024, 6144], P('ice', 'hyd'), may hold values 0 or 1
- float_mask: int32 [1024, 6144], P('ice', 'hyd'), may hold values 0 or 1
- friction: float32 [1024, 6144], P('ice', 'hyd'), may hold values from 1 to 10
- geothermal: float32 [1024, 6144], P('ice', 'hyd'), may hold values from 0.2 to 2
- potential_prev: float32 [1024, 6144], P(('ice', 'hyd')), may hold values from 0.5 to 2.5
- overburden: float32 [1024, 6144], P(('ice', 'hyd')), may hold values from 1.5 to 3.5
- sheet_thick: float32 [1024, 6144], P(('ice', 'hyd')), may hold values from 0.05 to 0.5
- channel_east: int32 [1024, 6144], P(('ice', 'hyd')), may hold values 0 or 1
- channel_south: int32 [1024, 6144], P(('ice', 'hyd')), may hold values 0 or 1
- channel_area: float32 [1024, 6144], P(('ice', 'hyd')), may hold values from 0.2 to 2
Outputs:
- velocity: float32 [2, 20, 1024, 6144], P(None, None, 'ice', 'hyd')
- effective_pressure: float32 [1024, 6144], P('ice', 'hyd')
- potential: float32 [1024, 6144], P(('ice', 'hyd'))
- sheet_next: float32 [1024, 6144], P(('ice', 'hyd'))
The draws below stay inside these ranges and needn't reach their ends.
All inputs are finite; a program needn't handle non-finite values. No bound on the sum of `ice_mask` or of `float_mask` or of `channel_east` or of `channel_south` on one device may be relied on, other than what follows from the above.
Results may differ from the reference program's by a relative error of at most 0.0004.
Values may be sent and summed in bfloat16 or wider, within the bound.
No kernel may reach another device: no remote copies, remote signals or barrier semaphores. Data moves between devices by JAX's collectives and lax.ppermute only.
A program may use at most 192 MiB of HBM per device.

```python
import math
import jax
import jax.numpy as jnp

LAYERS = 20
KRYLOV = 2
HYD_ITERS = 3
NY = 1024
NX = 6144


def draw_driving_stress(key, part):
    noise_key, row_key, col_key = jax.random.split(key, 3)
    row_ramp = 1.0 + 2.0 * jnp.arange(NY, dtype=jnp.float32) / NY
    row_scale = 10.0 ** jax.random.uniform(row_key, (NY,), jnp.float32, -0.5, 0.5)
    col_scale = 10.0 ** jax.random.uniform(col_key, (NX,), jnp.float32, -0.5, 0.5)
    noise = jnp.clip(jax.random.normal(noise_key, (2, NY, NX), jnp.float32), -4.0, 4.0)
    return noise * (row_ramp * row_scale)[None, :, None] * col_scale[None, None, :]


def set_ends(entries, rng, low, top_value):
    place = [jax.random.randint(jax.random.fold_in(rng, axis), (), 0, length) for axis, length in enumerate(entries.shape)]
    longest = entries.shape.index(max(entries.shape))
    neighbour = place[:longest] + [(place[longest] + 1) % entries.shape[longest]] + place[longest + 1:]
    return entries.at[tuple(place)].set(low).at[tuple(neighbour)].set(top_value)


def levels(own_key, dims, shards, low, high):
    gain = 1.0
    for position, parts in shards:
        heights = jax.random.uniform(jax.random.fold_in(jax.random.fold_in(own_key, 6), position), (parts,), jnp.float32, low / len(shards), high / len(shards))
        gain = gain * jnp.repeat(jnp.exp(heights), dims[position] // parts).reshape((-1,) + (1,) * (len(dims) - 1 - position))
    return gain


def setup_inputs(seed: int = 0) -> dict:
    arg_keys = jax.random.split(jax.random.key(seed), 13)
    viscosity = jnp.clip(jnp.exp(math.log(3.0) - 2.306499 * jax.random.uniform(arg_keys[0], (LAYERS, NY, NX), jnp.float32) ** levels(arg_keys[0], (LAYERS, NY, NX), ((1, 64), (2, 2)), -0.2, 0.2)), 0.29882812, 3.0).astype(jnp.bfloat16)
    driving_stress = draw_driving_stress(jax.random.fold_in(arg_keys[12], 71), 0)
    ice_mask = set_ends((jax.random.randint(arg_keys[2], (NY, NX), 0, 8) < 7).astype(jnp.int32), jax.random.fold_in(arg_keys[2], 1), 0, 1)
    float_mask = set_ends((jax.random.randint(arg_keys[3], (NY, NX), 0, 4) < 1).astype(jnp.int32), jax.random.fold_in(arg_keys[3], 1), 0, 1)
    friction = jnp.clip(jnp.exp(math.log(10.0) - 2.3025851 * jax.random.uniform(arg_keys[4], (NY, NX), jnp.float32) ** levels(arg_keys[4], (NY, NX), ((0, 64), (1, 2)), -0.2, 0.2)), 1.0, 10.0)
    geothermal = jnp.clip(jnp.exp(math.log(2.0) - 2.3025851 * jax.random.uniform(arg_keys[5], (NY, NX), jnp.float32) ** levels(arg_keys[5], (NY, NX), ((0, 64), (1, 2)), -0.2, 0.2)), 0.2, 2.0)
    potential_prev = jnp.clip(0.5 + 2.0 * jax.random.uniform(arg_keys[6], (NY, NX), jnp.float32) ** levels(arg_keys[6], (NY, NX), ((0, 128),), -0.2, 0.2), 0.5, 2.5)
    overburden = jnp.clip(1.5 + 2.0 * jax.random.uniform(arg_keys[7], (NY, NX), jnp.float32) ** levels(arg_keys[7], (NY, NX), ((0, 128),), -0.2, 0.2), 1.5, 3.5)
    sheet_thick = jnp.clip(jnp.exp(math.log(0.5) - 2.3025851 * jax.random.uniform(arg_keys[8], (NY, NX), jnp.float32) ** levels(arg_keys[8], (NY, NX), ((0, 128),), -0.2, 0.2)), 0.05, 0.5)
    channel_east = set_ends((jax.random.randint(arg_keys[9], (NY, NX), 0, 3) < 1).astype(jnp.int32), jax.random.fold_in(arg_keys[9], 1), 0, 1)
    channel_south = set_ends((jax.random.randint(arg_keys[10], (NY, NX), 0, 3) < 1).astype(jnp.int32), jax.random.fold_in(arg_keys[10], 1), 0, 1)
    channel_area = jnp.clip(jnp.exp(math.log(2.0) - 2.3025851 * jax.random.uniform(arg_keys[11], (NY, NX), jnp.float32) ** levels(arg_keys[11], (NY, NX), ((0, 128),), -0.2, 0.2)), 0.2, 2.0)
    return {"viscosity": viscosity, "driving_stress": driving_stress, "ice_mask": ice_mask, "float_mask": float_mask, "friction": friction, "geothermal": geothermal, "potential_prev": potential_prev, "overburden": overburden, "sheet_thick": sheet_thick, "channel_east": channel_east, "channel_south": channel_south, "channel_area": channel_area}


vertical_weight = 4.0
relax_weight = 0.1
melt_factor = 0.5
sheet_conduct = 2.0
channel_conduct = 1.5
storage = 1.0
bump_height = 0.3
time_step = 0.5
speed_floor = 0.25

def faces_from(padded):
    center = padded[:, 1:-1, 1:-1]
    east_face = jnp.sqrt(center * padded[:, 1:-1, 2:])
    west_face = jnp.sqrt(center * padded[:, 1:-1, :-2])
    south_face = jnp.sqrt(center * padded[:, 2:, 1:-1])
    north_face = jnp.sqrt(center * padded[:, :-2, 1:-1])
    upward = jnp.sqrt(center[1:] * center[:-1])
    return (east_face, west_face, south_face, north_face, upward)

def one_component(padded, face_set, diagonal, col_factor, row_factor):
    east_face, west_face, south_face, north_face, upward = face_set
    center = padded[:, 1:-1, 1:-1]
    along_cols = east_face * (center - padded[:, 1:-1, 2:]) + west_face * (center - padded[:, 1:-1, :-2])
    along_rows = south_face * (center - padded[:, 2:, 1:-1]) + north_face * (center - padded[:, :-2, 1:-1])
    vertical_flux = upward * (center[1:] - center[:-1])
    vertical = jnp.pad(vertical_flux, ((1, 0), (0, 0), (0, 0))) - jnp.pad(vertical_flux, ((0, 1), (0, 0), (0, 0)))
    return diagonal * center + col_factor * along_cols + row_factor * along_rows + vertical_weight * vertical

def apply_operator(padded, face_set, diagonal):
    first = one_component(padded[0], face_set, diagonal, 4.0, 1.0)
    second = one_component(padded[1], face_set, diagonal, 1.0, 4.0)
    return jnp.stack([first, second])

def sweep(padded, east_face, west_face, south_face, north_face, fixed_part, overburden, sheet_thick):
    current = padded[1:-1]
    right_value = jnp.pad(current[:, 1:], ((0, 0), (0, 1)))
    left_value = jnp.pad(current[:, :-1], ((0, 0), (1, 0)))
    gathered = east_face * right_value + west_face * left_value + south_face * padded[2:] + north_face * padded[:-2]
    conduct_sum = east_face + west_face + south_face + north_face
    creep_rate = sheet_thick * jnp.abs(overburden - current)
    return (fixed_part + creep_rate * overburden + gathered) / (storage + creep_rate + conduct_sum)

def reference(viscosity, driving_stress, ice_mask, float_mask, friction, geothermal, potential_prev, overburden, sheet_thick, channel_east, channel_south, channel_area):
    ice_cover = ice_mask.astype(jnp.float32)
    grounded = ice_cover * (1.0 - float_mask.astype(jnp.float32))
    weight = viscosity.astype(jnp.float32) * ice_cover[None]
    face_set = faces_from(jnp.pad(weight, ((0, 0), (1, 1), (1, 1))))
    bottom = (jnp.arange(LAYERS) == 0).astype(jnp.float32)[:, None, None]
    diagonal = (1.0 - ice_cover + relax_weight * ice_cover)[None] + bottom * (friction * grounded)[None]
    forcing = jnp.broadcast_to((driving_stress * ice_cover[None])[:, None], (2, LAYERS) + ice_cover.shape)
    solution = jnp.zeros(forcing.shape, jnp.float32)
    residual = forcing
    direction = forcing
    norm_now = jnp.sum(residual * residual)
    for iteration in range(KRYLOV):
        padded = jnp.pad(direction, ((0, 0), (0, 0), (1, 1), (1, 1)))
        applied = apply_operator(padded, face_set, diagonal)
        step_size = norm_now / jnp.sum(direction * applied)
        solution = solution + step_size * direction
        residual = residual - step_size * applied
        norm_next = jnp.sum(residual * residual)
        direction = residual + norm_next / norm_now * direction
        norm_now = norm_next
    slide_sq = solution[0, 0] * solution[0, 0] + solution[1, 0] * solution[1, 0]
    slide_speed = jnp.sqrt(slide_sq + speed_floor)
    melt_rate = melt_factor * (geothermal + friction * grounded * slide_sq)
    east_face = sheet_conduct * sheet_thick + channel_conduct * channel_east.astype(jnp.float32) * channel_area
    south_face = sheet_conduct * sheet_thick + channel_conduct * channel_south.astype(jnp.float32) * channel_area
    west_face = jnp.pad(east_face[:, :-1], ((0, 0), (1, 0)))
    north_face = jnp.pad(south_face[:-1], ((1, 0), (0, 0)))
    opening = slide_speed * jnp.maximum(bump_height - sheet_thick, 0.0)
    fixed_part = storage * potential_prev + melt_rate - opening
    potential = potential_prev
    for iteration in range(HYD_ITERS):
        padded_rows = jnp.pad(potential, ((1, 1), (0, 0)))
        potential = sweep(padded_rows, east_face, west_face, south_face, north_face, fixed_part, overburden, sheet_thick)
    pressure = overburden - potential
    sheet_next = sheet_thick + time_step * (opening - sheet_thick * jnp.abs(pressure) * pressure)
    return (solution, pressure, potential, sheet_next)
```

```python
import functools

import jax
import jax.numpy as jnp
from jax import lax
from jax.experimental import pallas as pl
from jax.experimental.pallas import tpu as pltpu
from jax.sharding import PartitionSpec as P

HYD_ITERS = 3
vertical_weight = 4.0
relax_weight = 0.1
melt_factor = 0.5
sheet_conduct = 2.0
channel_conduct = 1.5
storage = 1.0
bump_height = 0.3
time_step = 0.5
speed_floor = 0.25

AXES = ("ice", "hyd")
F32 = jnp.float32
LANES = 128
CHUNK = 512
FACTORS = ((4.0, 1.0), (1.0, 4.0))
FIELDS = 24
F0, FG, MASK = 20, 22, 23


def whole(space=pltpu.VMEM):
    return pl.BlockSpec(memory_space=space)


def shape_of(*dims):
    return jax.ShapeDtypeStruct(dims, F32)


def lane_index(rows, cols):
    return lax.broadcasted_iota(jnp.int32, (rows, cols), 1)


def row_index(rows, cols):
    return lax.broadcasted_iota(jnp.int32, (rows, cols), 0)


def east_of(value, right):
    cols = value.shape[1]
    joined = jnp.concatenate([value, right], axis=1)
    return pltpu.roll(joined, cols + LANES - 1, 1)[:, :cols]


def west_of(value, left):
    joined = jnp.concatenate([left, value], axis=1)
    return pltpu.roll(joined, 1, 1)[:, LANES:]


def south_of(value, below):
    rows, cols = value.shape
    return jnp.where(row_index(rows, cols) == rows - 1, below, pltpu.roll(value, rows - 1, 0))


def north_of(value, above):
    rows, cols = value.shape
    return jnp.where(row_index(rows, cols) == 0, above, pltpu.roll(value, 1, 0))


def root(weight):
    weight = weight.astype(F32)
    return weight * lax.rsqrt(weight)


def edge_kernel(half, visc, drive, mask, floating, friction, force, fric, message):
    layers, rows, cols = visc.shape
    cover = mask[...].astype(F32)
    grounded = cover * (1.0 - floating[...].astype(F32))
    fric[...] = friction[...] * grounded
    for comp in range(2):
        force[comp] = drive[comp] * cover
    left_half = half[0] == 0
    first = jnp.where(left_half, LANES - 2, 0)
    lane = lane_index(rows, LANES)
    keep = (lane >= first) & (lane < first + 2)

    def edge(read):
        return jnp.where(left_half, read(slice(cols - LANES, cols)), read(slice(0, LANES)))

    edge_cover = edge(lambda part: mask[:, part]).astype(F32)
    fields = [
        root(edge(lambda part, layer=layer: visc[layer, :, part].astype(F32))) * edge_cover
        for layer in range(layers)
    ]
    fields += [edge(lambda part, comp=comp: force[comp, :, part]) for comp in range(2)]
    fields += [edge(lambda part: fric[:, part]), edge_cover]
    total = jnp.zeros((rows, LANES), F32)
    for index, field in enumerate(fields):
        part = jnp.where(keep, field, 0.0)
        total += pltpu.roll(part, 2 * index, 1) if index else part
    message[...] = total


def root_kernel(visc, mask, force, fric, roots, lines):
    layers, rows, cols = visc.shape
    for start in range(0, cols, CHUNK):
        part = slice(start, start + CHUNK)
        cover = mask[:, part].astype(F32)

        def step(layer, carry, part=part, cover=cover):
            value = root(visc[layer, :, part]) * cover
            roots[layer, :, part] = value
            for slot, row in enumerate((0, 1, rows - 1)):
                lines[slot, pl.ds(layer, 1), part] = value[row : row + 1]
            return carry

        lax.fori_loop(0, layers, step, 0, unroll=2)
        for slot, row in enumerate((0, 1, rows - 1)):
            for comp in range(2):
                lines[slot, F0 + comp : F0 + comp + 1, part] = force[comp, row : row + 1, part]
            lines[slot, FG : FG + 1, part] = fric[row : row + 1, part]
            lines[slot, MASK : MASK + 1, part] = cover[row : row + 1]


def unpack_kernel(half, message, lines, block, to_south, to_north):
    rows = message.shape[0]
    cols = lines.shape[2]
    first = jnp.where(half[0] == 0, 0, LANES - 2)
    lane = lane_index(rows, LANES)
    keep = (lane >= first) & (lane < first + 2)
    packed = message[...]
    to_north[:, :, :cols] = lines[0:2]
    to_south[:, :cols] = lines[2]
    for index in range(FIELDS):
        part = pltpu.roll(packed, LANES - 2 * index, 1) if index else packed
        part = jnp.where(keep, part, 0.0)
        block[index] = part
        to_north[0, index : index + 1, cols:] = part[0:1]
        to_north[1, index : index + 1, cols:] = part[1:2]
        to_south[index : index + 1, cols:] = part[rows - 1 : rows]


def line_of(ref, layer, start, size):
    if size > LANES:
        return ref[pl.ds(layer, 1), start : start + size]
    return ref[pl.ds(layer, 1), start - LANES : start + size][:, LANES:]


def fold(value):
    total = None
    for row in range(0, value.shape[0], 8):
        for col in range(0, value.shape[1], LANES):
            part = value[row : row + 8, col : col + LANES]
            total = part if total is None else total + part
    return total


def relax(cover):
    return (1.0 - cover) + relax_weight * cover


def operator_kernel(
    roots, force, fric, mask, block, above, below, lines, image, sums, slopes, scaled, diag, line, edge
):
    layers, rows, cols = roots.shape
    chunks = [(start, CHUNK) for start in range(0, cols, CHUNK)]

    def columns(read_own, read_block, start, size):
        if start == cols:
            return read_block(), read_own(slice(cols - LANES, cols)), jnp.zeros((rows, LANES), F32)
        left = read_own(slice(start - LANES, start)) if start else read_block()
        stop = start + size
        right = read_own(slice(stop, stop + LANES)) if stop < cols else read_block()
        return read_own(slice(start, stop)), left, right

    squares = jnp.zeros((8, LANES), F32)
    for start, size in chunks + [(cols, LANES)]:
        part = slice(start, start + size)
        own = start < cols
        cover = mask[:, part].astype(F32) if own else block[MASK]
        drag = fric[:, part] if own else block[FG]
        plain = relax(cover)
        if own:
            diag[0, :, part] = plain
            diag[1, :, part] = plain + drag
        for comp, (col_factor, row_factor) in enumerate(FACTORS):
            here, left, right = columns(
                lambda cut, comp=comp: force[comp, :, cut], lambda comp=comp: block[F0 + comp], start, size
            )
            up = above[F0 + comp : F0 + comp + 1, part]
            down = below[0, F0 + comp : F0 + comp + 1, part]
            slopes[4 * comp, :, part] = col_factor * (here - east_of(here, right))
            slopes[4 * comp + 1, :, part] = col_factor * (here - west_of(here, left))
            slopes[4 * comp + 2, :, part] = row_factor * (here - south_of(here, down))
            slopes[4 * comp + 3, :, part] = row_factor * (here - north_of(here, up))
            scaled[0, comp, :, part] = plain * here
            scaled[1, comp, :, part] = (plain + drag) * here
            if own:
                squares += fold(here * here)

    for start, size in chunks:
        part = slice(start, start + size)
        stop = start + size
        before = slice(start - LANES, start) if start else slice(cols, cols + LANES)
        after = slice(stop, stop + LANES)
        here = below[0, 0:layers, part]
        east = here * east_of(here, below[0, 0:layers, after])
        west = here * west_of(here, below[0, 0:layers, before])
        south = here * below[1, 0:layers, part]
        north = here * lines[2, 0:layers, part]
        cover = below[0, MASK : MASK + 1, part]
        lowest = jnp.where(row_index(layers, size) == 0, below[0, FG : FG + 1, part], 0.0)
        full = relax(cover) + lowest
        for comp, (col_factor, row_factor) in enumerate(FACTORS):
            row = slice(F0 + comp, F0 + comp + 1)
            mid = below[0, row, part]
            line[comp, 0:layers, part] = full * mid + (
                col_factor
                * (
                    east * (mid - east_of(mid, below[0, row, after]))
                    + west * (mid - west_of(mid, below[0, row, before]))
                )
                + row_factor
                * (south * (mid - below[1, row, part]) + north * (mid - lines[2, row, part]))
            )

    def layer_step(layer, carry):
        kind = jnp.where(layer == 0, 1, 0)
        lower = jnp.maximum(layer - 1, 0)
        for start, size in chunks + [(cols, LANES)]:
            part = slice(start, start + size)
            here, left, right = columns(
                lambda cut: roots[layer, :, cut], lambda: block[layer], start, size
            )
            east = east_of(here, right)
            west = west_of(here, left)
            south = south_of(here, line_of(below.at[0], layer, start, size))
            north = north_of(here, line_of(above, layer, start, size))
            for comp in range(2):
                flux = (
                    east * slopes[4 * comp, :, part]
                    + west * slopes[4 * comp + 1, :, part]
                    + south * slopes[4 * comp + 2, :, part]
                    + north * slopes[4 * comp + 3, :, part]
                )
                value = scaled[kind, comp, :, part] + here * flux
                if start < cols:
                    image[comp, layer, :, part] = value
                else:
                    edge[comp] = value
        cross, square, energy = carry
        for start, size in chunks:
            part = slice(start, start + size)
            stop = start + size
            here = roots[layer, :, part]
            right = roots[layer, :, stop : stop + LANES] if stop < cols else block[layer]
            east = east_of(here, right)
            south = south_of(here, line_of(below.at[0], layer, start, size))
            beneath = roots[lower, :, part]
            to_east, to_south, to_lower, size_sq, product = 0.0, 0.0, 0.0, 0.0, 0.0
            for comp, (col_factor, row_factor) in enumerate(FACTORS):
                value = image[comp, layer, :, part]
                right = image[comp, layer, :, stop : stop + LANES] if stop < cols else edge[comp]
                step = value - east_of(value, right)
                step = step * step
                to_east += step if col_factor == 1.0 else col_factor * step
                step = value - south_of(value, line_of(line.at[comp], layer, start, size))
                step = step * step
                to_south += step if row_factor == 1.0 else row_factor * step
                step = value - image[comp, lower, :, part]
                to_lower += step * step
                size_sq += value * value
                product += value * force[comp, :, part]
            faces = here * (east * to_east + south * to_south + beneath * (vertical_weight * to_lower))
            cross += fold(product)
            square += fold(size_sq)
            energy += fold(faces + diag[kind, :, part] * size_sq)
        return cross, square, energy

    zero = jnp.zeros((8, LANES), F32)
    cross, square, energy = lax.fori_loop(0, layers, layer_step, (zero, zero, zero))
    lane = lane_index(8, LANES)
    packed = jnp.zeros((8, LANES), F32)
    for index, part in enumerate((layers * squares, cross, square, energy)):
        packed = jnp.where(lane == index, jnp.sum(part), packed)
    sums[...] = packed


def velocity_kernel(weights, force, image, out, staged, done):
    layers = image.shape[1]
    first, second = weights[0], weights[1]

    def copy(layer):
        return pltpu.make_async_copy(staged.at[:, layer], out.at[:, layer], done.at[layer])

    def step(layer, carry):
        for comp in range(2):
            staged[comp, layer] = first * force[comp] + second * image[comp, layer]
        copy(layer).start()
        return carry

    lax.fori_loop(0, layers, step, 0)

    def finish(layer, carry):
        copy(layer).wait()
        return carry

    lax.fori_loop(0, layers, finish, 0)


def call(kernel, out_shape, n_in, scratch=(), smem=(), out_space=pltpu.VMEM, **kwargs):
    outs = out_shape if isinstance(out_shape, (list, tuple)) else (out_shape,)
    specs = tuple(whole(out_space) for _ in outs)
    return pl.pallas_call(
        kernel,
        out_shape=out_shape,
        in_specs=[whole(pltpu.SMEM) if i in smem else whole() for i in range(n_in)],
        out_specs=specs if isinstance(out_shape, (list, tuple)) else specs[0],
        scratch_shapes=list(scratch),
        compiler_params=pltpu.CompilerParams(vmem_limit_bytes=48 << 20),
        **kwargs,
    )


def moved(value, axis, steps):
    count = lax.axis_size(axis)
    leading, last = (max(0, -steps), min(count, count - steps))
    return lax.ppermute(value, axis, [(source, source + steps) for source in range(leading, last)])


def with_rows(cells):
    return jnp.concatenate([moved(cells[-1:], AXES, 1), cells, moved(cells[:1], AXES, -1)], axis=0)


def sweep(padded, east_face, west_face, south_face, north_face, fixed_part, overburden, sheet_thick):
    current = padded[1:-1]
    right_value = jnp.pad(current[:, 1:], ((0, 0), (0, 1)))
    left_value = jnp.pad(current[:, :-1], ((0, 0), (1, 0)))
    gathered = (
        east_face * right_value
        + west_face * left_value
        + south_face * padded[2:]
        + north_face * padded[:-2]
    )
    conduct_sum = east_face + west_face + south_face + north_face
    creep_rate = sheet_thick * jnp.abs(overburden - current)
    return (fixed_part + creep_rate * overburden + gathered) / (storage + creep_rate + conduct_sum)


def body(
    viscosity,
    driving_stress,
    ice_mask,
    float_mask,
    friction,
    geothermal,
    potential_prev,
    overburden,
    sheet_thick,
    channel_east,
    channel_south,
    channel_area,
):
    layers, rows, cols = viscosity.shape
    half = lax.axis_index("hyd").astype(jnp.int32)[None]
    swap = [(0, 1), (1, 0)]
    force, fric, message = call(
        edge_kernel, [shape_of(2, rows, cols), shape_of(rows, cols), shape_of(rows, LANES)], 6, smem=(0,)
    )(half, viscosity, driving_stress, ice_mask, float_mask, friction)
    received = lax.ppermute(message, "hyd", swap)
    roots, lines = call(root_kernel, [shape_of(layers, rows, cols), shape_of(3, FIELDS, cols)], 4)(
        viscosity, ice_mask, force, fric
    )
    wide = cols + LANES
    block, to_south, to_north = call(
        unpack_kernel,
        [shape_of(FIELDS, rows, LANES), shape_of(FIELDS, wide), shape_of(2, FIELDS, wide)],
        3,
        smem=(0,),
    )(half, received, lines)
    above = moved(to_south, "ice", 1)
    below = moved(to_north, "ice", -1)
    image, sums = call(
        operator_kernel,
        [shape_of(2, layers, rows, cols), shape_of(8, LANES)],
        8,
        scratch=[
            pltpu.VMEM((8, rows, wide), F32),
            pltpu.VMEM((2, 2, rows, wide), F32),
            pltpu.VMEM((2, rows, cols), F32),
            pltpu.VMEM((2, FIELDS, cols), F32),
            pltpu.VMEM((2, rows, LANES), F32),
        ],
    )(roots, force, fric, ice_mask, block, above, below, lines)
    count = lax.axis_size("ice") * lax.axis_size("hyd")
    spread = jnp.broadcast_to(sums[0:1], (count, LANES))
    gathered = lax.all_to_all(spread, AXES, 0, 0, tiled=True)
    total = jnp.sum(gathered, axis=0)
    norm, cross, square, energy = total[0], total[1], total[2], total[3]
    step_one = norm / cross
    norm_next = step_one * (step_one * square - 2.0 * cross) + norm
    ratio = norm_next / norm
    lead = 1.0 + ratio
    curve = lead * lead * cross - 2.0 * lead * step_one * square + step_one * step_one * energy
    step_two = norm_next / curve
    weights = jnp.stack([step_one + step_two * lead, -step_two * step_one])
    velocity = pl.pallas_call(
        velocity_kernel,
        out_shape=shape_of(2, layers, rows, cols),
        in_specs=[whole(pltpu.SMEM), whole(), whole()],
        out_specs=whole(pl.ANY),
        scratch_shapes=[pltpu.VMEM((2, layers, rows, cols), F32), pltpu.SemaphoreType.DMA((layers,))],
        compiler_params=pltpu.CompilerParams(vmem_limit_bytes=48 << 20),
    )(weights, force, image)

    low = weights[0] * force + weights[1] * image[:, 0]
    slide_sq = low[0] * low[0] + low[1] * low[1]
    slide_speed = jnp.sqrt(slide_sq + speed_floor)
    melt_rate = melt_factor * (geothermal + fric * slide_sq)
    pair = jnp.stack([melt_rate, slide_speed])
    strip_rows = rows // 2
    is_left = half[0] == 0
    mine = jnp.where(is_left, pair[:, :strip_rows], pair[:, strip_rows:])
    theirs = jnp.where(is_left, pair[:, strip_rows:], pair[:, :strip_rows])
    theirs = lax.ppermute(theirs, "hyd", swap)
    strip = jnp.concatenate(
        [jnp.where(is_left, mine, theirs), jnp.where(is_left, theirs, mine)], axis=2
    )
    melt_strip, speed_strip = strip[0], strip[1]
    east_face = sheet_conduct * sheet_thick + channel_conduct * channel_east.astype(F32) * channel_area
    south_face = sheet_conduct * sheet_thick + channel_conduct * channel_south.astype(F32) * channel_area
    west_face = jnp.pad(east_face[:, :-1], ((0, 0), (1, 0)))
    north_face = jnp.concatenate([moved(south_face[-1:], AXES, 1), south_face[:-1]], axis=0)
    opening = speed_strip * jnp.maximum(bump_height - sheet_thick, 0.0)
    fixed_part = storage * potential_prev + melt_strip - opening
    potential = potential_prev
    for iteration in range(HYD_ITERS):
        potential = sweep(
            with_rows(potential),
            east_face,
            west_face,
            south_face,
            north_face,
            fixed_part,
            overburden,
            sheet_thick,
        )
    pressure = overburden - potential
    sheet_next = sheet_thick + time_step * (opening - sheet_thick * jnp.abs(pressure) * pressure)
    keep = jnp.where(is_left, pressure[:, :cols], pressure[:, cols:])
    give = jnp.where(is_left, pressure[:, cols:], pressure[:, :cols])
    got = lax.ppermute(give, "hyd", swap)
    effective = jnp.concatenate([jnp.where(is_left, keep, got), jnp.where(is_left, got, keep)], axis=0)
    return (velocity, effective, potential, sheet_next)


def solution(mesh):
    tiles = P("ice", "hyd")
    layered = P(None, "ice", "hyd")
    strips = P(("ice", "hyd"), None)
    return jax.shard_map(
        body,
        mesh=mesh,
        in_specs=(layered, layered, tiles, tiles, tiles, tiles) + (strips,) * 6,
        out_specs=(P(None, None, "ice", "hyd"), tiles, strips, strips),
        check_vma=False,
    )
```

```python
import functools

import jax
import jax.numpy as jnp
from jax import lax
from jax.experimental import pallas as pl
from jax.experimental.pallas import tpu as pltpu
from jax.sharding import PartitionSpec as P

HYD_ITERS = 3
vertical_weight = 4.0
relax_weight = 0.1
melt_factor = 0.5
sheet_conduct = 2.0
channel_conduct = 1.5
storage = 1.0
bump_height = 0.3
time_step = 0.5
speed_floor = 0.25

AXES = ("ice", "hyd")
F32 = jnp.float32
LANES = 128
CHUNK = 512
FETCH = 1536
FACTORS = ((4.0, 1.0), (1.0, 4.0))
FIELDS = 24
F0, FG, MASK = 20, 22, 23


def whole(space=pltpu.VMEM):
    return pl.BlockSpec(memory_space=space)


def shape_of(*dims):
    return jax.ShapeDtypeStruct(dims, F32)


def lane_index(rows, cols):
    return lax.broadcasted_iota(jnp.int32, (rows, cols), 1)


def row_index(rows, cols):
    return lax.broadcasted_iota(jnp.int32, (rows, cols), 0)


def east_of(value, right):
    cols = value.shape[1]
    joined = jnp.concatenate([value, right], axis=1)
    return pltpu.roll(joined, cols + LANES - 1, 1)[:, :cols]


def west_of(value, left):
    joined = jnp.concatenate([left, value], axis=1)
    return pltpu.roll(joined, 1, 1)[:, LANES:]


def south_of(value, below):
    rows, cols = value.shape
    return jnp.where(row_index(rows, cols) == rows - 1, below, pltpu.roll(value, rows - 1, 0))


def north_of(value, above):
    rows, cols = value.shape
    return jnp.where(row_index(rows, cols) == 0, above, pltpu.roll(value, 1, 0))


def root(weight):
    weight = weight.astype(F32)
    return weight * lax.rsqrt(weight)


def edge_kernel(half, visc, drive, mask, floating, friction, message, w, d, m, fl, fr, done):
    layers, rows, cols = visc.shape
    left_half = half[0] == 0
    start = pl.multiple_of(jnp.where(left_half, cols - LANES, 0), LANES)
    cut = pl.ds(start, LANES)
    copies = [
        pltpu.make_async_copy(source.at[..., cut], target, done.at[index])
        for index, (source, target) in enumerate(
            ((visc, w), (drive, d), (mask, m), (floating, fl), (friction, fr))
        )
    ]
    for copy in copies:
        copy.start()
    for copy in copies:
        copy.wait()
    first = jnp.where(left_half, LANES - 2, 0)
    lane = lane_index(rows, LANES)
    keep = (lane >= first) & (lane < first + 2)
    cover = m[...].astype(F32)
    fields = [root(w[layer]) * cover for layer in range(layers)]
    fields += [d[comp] * cover for comp in range(2)]
    fields += [fr[...] * (cover * (1.0 - fl[...].astype(F32))), cover]
    total = jnp.zeros((rows, LANES), F32)
    for index, field in enumerate(fields):
        part = jnp.where(keep, field, 0.0)
        total += pltpu.roll(part, 2 * index, 1) if index else part
    message[...] = total


def root_kernel(
    visc, drive, mask, floating, friction, roots, lines, force, fric, covers, w, d, m, fl, fr, done
):
    layers, rows, cols = visc.shape
    starts = list(range(0, cols, FETCH))

    def copies(index):
        part = slice(starts[index], starts[index] + FETCH)
        return [
            pltpu.make_async_copy(source.at[..., part], target.at[..., part], done.at[index, slot])
            for slot, (source, target) in enumerate(
                ((visc, w), (drive, d), (mask, m), (floating, fl), (friction, fr))
            )
        ]

    for index in range(len(starts)):
        for copy in copies(index):
            copy.start()
    for index, begin in enumerate(starts):
        for copy in copies(index):
            copy.wait()
        for start in range(begin, begin + FETCH, CHUNK):
            part = slice(start, start + CHUNK)
            cover = m[:, part].astype(F32)
            grounded = cover * (1.0 - fl[:, part].astype(F32))
            drag = fr[:, part] * grounded
            fric[:, part] = drag
            covers[:, part] = cover
            pushes = [d[comp, :, part] * cover for comp in range(2)]
            for comp in range(2):
                force[comp, :, part] = pushes[comp]

            def step(layer, carry, part=part, cover=cover):
                value = root(w[layer, :, part]) * cover
                roots[layer, :, part] = value
                for slot, row in enumerate((0, 1, rows - 1)):
                    lines[slot, pl.ds(layer, 1), part] = value[row : row + 1]
                return carry

            lax.fori_loop(0, layers, step, 0, unroll=2)
            for slot, row in enumerate((0, 1, rows - 1)):
                for comp in range(2):
                    lines[slot, F0 + comp : F0 + comp + 1, part] = pushes[comp][row : row + 1]
                lines[slot, FG : FG + 1, part] = drag[row : row + 1]
                lines[slot, MASK : MASK + 1, part] = cover[row : row + 1]


def unpack_kernel(half, message, lines, fringe, block, to_south, to_north):
    rows = message.shape[0]
    cols = lines.shape[2]
    first = jnp.where(half[0] == 0, 0, LANES - 2)
    lane = lane_index(rows, LANES)
    keep = (lane >= first) & (lane < first + 2)
    packed = message[...]
    to_north[0:FIELDS, :cols] = lines[0]
    to_north[FIELDS : 2 * FIELDS, :cols] = lines[1]
    to_north[2 * FIELDS :, :cols] = fringe[0]
    to_south[0:FIELDS, :cols] = lines[2]
    to_south[FIELDS:, :cols] = fringe[1]
    to_north[2 * FIELDS :, cols:] = jnp.zeros((16, LANES), F32)
    to_south[FIELDS:, cols:] = jnp.zeros((16, LANES), F32)
    for index in range(FIELDS):
        part = pltpu.roll(packed, LANES - 2 * index, 1) if index else packed
        part = jnp.where(keep, part, 0.0)
        block[index] = part
        to_north[index : index + 1, cols:] = part[0:1]
        to_north[FIELDS + index : FIELDS + index + 1, cols:] = part[1:2]
        to_south[index : index + 1, cols:] = part[rows - 1 : rows]


def line_of(ref, layer, start, size):
    if size > LANES:
        return ref[pl.ds(layer, 1), start : start + size]
    return ref[pl.ds(layer, 1), start - LANES : start + size][:, LANES:]


def fold(value):
    total = None
    for row in range(0, value.shape[0], 8):
        for col in range(0, value.shape[1], LANES):
            part = value[row : row + 8, col : col + LANES]
            total = part if total is None else total + part
    return total


def relax(cover):
    return (1.0 - cover) + relax_weight * cover


def operator_kernel(
    roots, force, fric, mask, block, above, below, lines, image, sums, slopes, scaled, diag, line, edge
):
    layers, rows, cols = roots.shape
    chunks = [(start, CHUNK) for start in range(0, cols, CHUNK)]

    def columns(read_own, read_block, start, size):
        if start == cols:
            return read_block(), read_own(slice(cols - LANES, cols)), jnp.zeros((rows, LANES), F32)
        left = read_own(slice(start - LANES, start)) if start else read_block()
        stop = start + size
        right = read_own(slice(stop, stop + LANES)) if stop < cols else read_block()
        return read_own(slice(start, stop)), left, right

    squares = jnp.zeros((8, LANES), F32)
    for start, size in chunks + [(cols, LANES)]:
        part = slice(start, start + size)
        own = start < cols
        cover = mask[:, part] if own else block[MASK]
        drag = fric[:, part] if own else block[FG]
        plain = relax(cover)
        if own:
            diag[0, :, part] = plain
            diag[1, :, part] = plain + drag
        for comp, (col_factor, row_factor) in enumerate(FACTORS):
            here, left, right = columns(
                lambda cut, comp=comp: force[comp, :, cut], lambda comp=comp: block[F0 + comp], start, size
            )
            up = above[F0 + comp : F0 + comp + 1, part]
            down = below[F0 + comp : F0 + comp + 1, part]
            slopes[4 * comp, :, part] = col_factor * (here - east_of(here, right))
            slopes[4 * comp + 1, :, part] = col_factor * (here - west_of(here, left))
            slopes[4 * comp + 2, :, part] = row_factor * (here - south_of(here, down))
            slopes[4 * comp + 3, :, part] = row_factor * (here - north_of(here, up))
            scaled[0, comp, :, part] = plain * here
            scaled[1, comp, :, part] = (plain + drag) * here
            if own:
                squares += fold(here * here)

    for start, size in chunks:
        part = slice(start, start + size)
        stop = start + size
        before = slice(start - LANES, start) if start else slice(cols, cols + LANES)
        after = slice(stop, stop + LANES)
        here = below[0:layers, part]
        east = here * east_of(here, below[0:layers, after])
        west = here * west_of(here, below[0:layers, before])
        south = here * below[FIELDS : FIELDS + layers, part]
        north = here * lines[2, 0:layers, part]
        cover = below[MASK : MASK + 1, part]
        drag = jnp.where(row_index(layers, size) == 0, below[FG : FG + 1, part], 0.0)
        full = relax(cover) + drag
        for comp, (col_factor, row_factor) in enumerate(FACTORS):
            row = slice(F0 + comp, F0 + comp + 1)
            under = slice(FIELDS + F0 + comp, FIELDS + F0 + comp + 1)
            mid = below[row, part]
            line[comp, 0:layers, part] = full * mid + (
                col_factor
                * (
                    east * (mid - east_of(mid, below[row, after]))
                    + west * (mid - west_of(mid, below[row, before]))
                )
                + row_factor
                * (south * (mid - below[under, part]) + north * (mid - lines[2, row, part]))
            )

    def layer_step(layer, carry):
        kind = jnp.where(layer == 0, 1, 0)
        lower = jnp.maximum(layer - 1, 0)
        for start, size in chunks + [(cols, LANES)]:
            part = slice(start, start + size)
            here, left, right = columns(
                lambda cut: roots[layer, :, cut], lambda: block[layer], start, size
            )
            east = east_of(here, right)
            west = west_of(here, left)
            south = south_of(here, line_of(below, layer, start, size))
            north = north_of(here, line_of(above, layer, start, size))
            for comp in range(2):
                flux = (
                    east * slopes[4 * comp, :, part]
                    + west * slopes[4 * comp + 1, :, part]
                    + south * slopes[4 * comp + 2, :, part]
                    + north * slopes[4 * comp + 3, :, part]
                )
                value = scaled[kind, comp, :, part] + here * flux
                if start < cols:
                    image[comp, layer, :, part] = value
                else:
                    edge[comp] = value
        cross, square, energy = carry
        for start, size in chunks:
            part = slice(start, start + size)
            stop = start + size
            here = roots[layer, :, part]
            right = roots[layer, :, stop : stop + LANES] if stop < cols else block[layer]
            east = east_of(here, right)
            south = south_of(here, line_of(below, layer, start, size))
            beneath = roots[lower, :, part]
            to_east, to_south, to_lower, size_sq, product = 0.0, 0.0, 0.0, 0.0, 0.0
            for comp, (col_factor, row_factor) in enumerate(FACTORS):
                value = image[comp, layer, :, part]
                right = image[comp, layer, :, stop : stop + LANES] if stop < cols else edge[comp]
                step = value - east_of(value, right)
                step = step * step
                to_east += step if col_factor == 1.0 else col_factor * step
                step = value - south_of(value, line_of(line.at[comp], layer, start, size))
                step = step * step
                to_south += step if row_factor == 1.0 else row_factor * step
                step = value - image[comp, lower, :, part]
                to_lower += step * step
                size_sq += value * value
                product += value * force[comp, :, part]
            faces = here * (east * to_east + south * to_south + beneath * (vertical_weight * to_lower))
            cross += fold(product)
            square += fold(size_sq)
            energy += fold(faces + diag[kind, :, part] * size_sq)
        return cross, square, energy

    zero = jnp.zeros((8, LANES), F32)
    cross, square, energy = lax.fori_loop(0, layers, layer_step, (zero, zero, zero))
    lane = lane_index(1, LANES)
    packed = jnp.zeros((1, LANES), F32)
    for index, part in enumerate((layers * squares, cross, square, energy)):
        packed = jnp.where(lane == index, jnp.sum(part), packed)
    sums[...] = jnp.broadcast_to(packed[None], sums.shape)


def krylov_weights(gathered):
    total = jnp.sum(gathered, axis=0)
    lane = lane_index(1, LANES)

    def moment(index):
        return jnp.sum(jnp.where(lane == index, total, 0.0), axis=1, keepdims=True)

    norm, cross, square, energy = (moment(index) for index in range(4))
    step_one = norm / cross
    norm_next = step_one * (step_one * square - 2.0 * cross) + norm
    lead = 1.0 + norm_next / norm
    curve = lead * lead * cross - 2.0 * lead * step_one * square + step_one * step_one * energy
    step_two = norm_next / curve
    return step_one + step_two * lead, -step_two * step_one


def placed(value, source_row, target_row):
    rows, cols = value.shape
    moved_rows = pltpu.roll(value, (rows - source_row) % rows, 0) if source_row % rows else value
    kept = jnp.where(row_index(rows, cols) < 3, moved_rows, 0.0)
    return pltpu.roll(kept, target_row % rows, 0) if target_row % rows else kept


def strip_kernel(info, *refs):
    sources, outs = refs[:12], refs[12:17]
    own, tile, pair, cross, fringe = outs
    buffers, done = refs[17:29], refs[29]
    copies = [
        pltpu.make_async_copy(source.at[0] if slot == 6 else source, target, done.at[slot])
        for slot, (source, target) in enumerate(zip(sources, buffers))
    ]
    for copy in copies:
        copy.start()
    for copy in copies:
        copy.wait()
    prev, burden, sheet, chan_east, chan_south, area, w, d, m, fl, fr, geo = buffers
    left = info[0] == 0
    wide = prev.shape[1]
    cols = w.shape[1]
    half_cols = cols // 2
    for start in range(0, wide, CHUNK):
        part = slice(start, start + CHUNK)
        base = sheet_conduct * sheet[:, part]
        fields = [
            prev[:, part],
            burden[:, part],
            sheet[:, part],
            base + channel_conduct * chan_east[:, part].astype(F32) * area[:, part],
            base + channel_conduct * chan_south[:, part].astype(F32) * area[:, part],
        ]
        first, last = None, None
        for index, field in enumerate(fields):
            own[index, :, part] = field
            both = jnp.concatenate([field, field], axis=0)
            head, tail = placed(both, 0, 3 * index), placed(both, 5, 3 * index)
            first = head if first is None else first + head
            last = tail if last is None else last + tail
        pair[:, part] = jnp.where(left, last, first)
        cross[:, part] = jnp.where(left, first, last)
    for start in range(0, cols, CHUNK):
        part = slice(start, start + CHUNK)

        def shifted_part(offset, start=start):
            return slice(wide + offset + start, wide + offset + start + CHUNK)

        cover = m[:, part].astype(F32)
        fields = [
            root(w[:, part]) * cover,
            d[0, :, part] * cover,
            d[1, :, part] * cover,
            fr[:, part] * (cover * (1.0 - fl[:, part].astype(F32))),
            geo[:, part],
        ]
        first, last, middle, halves = None, None, None, []
        for index, field in enumerate(fields):
            tile[index, :, part] = field
            head, tail = placed(field, 0, 3 * index), placed(field, 13, 3 * index)
            inner = jnp.where(left, placed(field, 5, 3 * index), placed(field, 8, 3 * index))
            first = head if first is None else first + head
            last = tail if last is None else last + tail
            middle = inner if middle is None else middle + inner
            halves.append(jnp.where(left, field[8:16], field[0:8]))
        fringe[0, :, part] = first
        fringe[1, :, part] = last
        cross[:, shifted_part(0)] = jnp.where(left, first, last)
        pair[:, shifted_part(0)] = jnp.concatenate(halves[0:2], axis=0)
        pair[:, shifted_part(cols)] = jnp.concatenate(halves[2:4], axis=0)
        pair[:, shifted_part(2 * cols)] = middle
        row = 0 if start < half_cols else 8
        place = wide + 3 * cols + start % half_cols
        pair[row : row + 8, place : place + CHUNK] = halves[4]


def assemble_kernel(info, own, tile, pair, cross, above, below, low, plan, base, hyd):
    left = info[0] == 0
    wide = own.shape[2]
    cols = tile.shape[2]
    half_cols = cols // 2
    row = row_index(16, CHUNK)
    in_north = row >= 13
    in_south = (row >= 8) & (row <= 10)
    blank = jnp.zeros((8, CHUNK), F32)

    def circle(main, index, mine, theirs):
        north = jnp.where(left, theirs, mine)
        south = jnp.where(left, mine, theirs)
        north = pltpu.roll(north, (13 - 3 * index) % 16, 0)
        south = pltpu.roll(south, (8 - 3 * index) % 16, 0)
        both = jnp.concatenate([main, blank], axis=0)
        return jnp.where(in_north, north, jnp.where(in_south, south, both))

    for start in range(0, wide, CHUNK):
        part = slice(start, start + CHUNK)
        from_pair, from_cross = pair[:, part], cross[:, part]
        for index in range(5):
            hyd[index, :, part] = circle(own[index, :, part], index, from_pair, from_cross)
    for start in range(0, cols, CHUNK):
        part = slice(start, start + CHUNK)
        middle = pair[:, wide + 2 * cols + start : wide + 2 * cols + start + CHUNK]
        outer = cross[:, wide + start : wide + start + CHUNK]
        north, south = above[FIELDS : FIELDS + 16, part], below[2 * FIELDS : 2 * FIELDS + 16, part]
        replaced = (left & in_north) | (jnp.logical_not(left) & in_south)
        for index in range(5):
            field = tile[index, :, part]
            swapped = jnp.concatenate([field[8:16], field[0:8]], axis=0)
            here = jnp.where(left, field, swapped)
            fringe = jnp.where(
                left,
                pltpu.roll(north, (13 - 3 * index) % 16, 0),
                pltpu.roll(south, (8 - 3 * index) % 16, 0),
            )
            here = jnp.where(replaced, fringe, here)
            if index < 4:
                place = wide + (index // 2) * cols + start
                top = (index % 2) * 8
            else:
                place = wide + 3 * cols + start % half_cols
                top = 0 if start < half_cols else 8
            there = circle(pair[top : top + 8, place : place + CHUNK], index, middle, outer)
            base[index, :, part] = jnp.where(left, here, there)
            base[index, :, cols + start : cols + start + CHUNK] = jnp.where(left, there, here)

    def neighbours(ref, start):
        stop = start + CHUNK
        zero = jnp.zeros((16, LANES), F32)
        here = ref[:, start:stop]
        right = ref[:, stop : stop + LANES] if stop < wide else zero
        leftward = ref[:, start - LANES : start] if start else zero
        return here, east_of(here, right), west_of(here, leftward), pltpu.roll(here, 15, 0), pltpu.roll(here, 1, 0)

    for start in range(0, wide, CHUNK):
        part = slice(start, start + CHUNK)
        here, east, west, south, north = neighbours(base.at[0], start)
        drag = base[3, :, part]
        diagonal = relax(jnp.where(here > 0.0, 1.0, 0.0)) + drag
        for comp, (col_factor, row_factor) in enumerate(FACTORS):
            mid, mid_e, mid_w, mid_s, mid_n = neighbours(base.at[1 + comp], start)
            low[comp, :, part] = mid
            low[2 + comp, :, part] = diagonal * mid + here * (
                col_factor * (east * (mid - mid_e) + west * (mid - mid_w))
                + row_factor * (south * (mid - mid_s) + north * (mid - mid_n))
            )
        low[4, :, part] = drag
        low[5, :, part] = base[4, :, part]
        prev, prev_e, prev_w, prev_s, prev_n = neighbours(hyd.at[0], start)
        burden, sheet = hyd[1, :, part], hyd[2, :, part]
        to_east, _, to_west, _, _ = neighbours(hyd.at[3], start)
        to_south = hyd[4, :, part]
        to_north = pltpu.roll(to_south, 1, 0)
        total = storage + (to_east + to_west + to_south + to_north)
        creep = sheet * jnp.abs(burden - prev)
        known = storage * prev + creep * burden
        known += to_east * prev_e + to_west * prev_w + to_south * prev_s + to_north * prev_n
        for index, value in enumerate(
            (storage * prev, burden, sheet, to_east, to_west, to_south, to_north, total, known, total + creep)
        ):
            plan[index, :, part] = value


def hydrology_kernel(info, gathered, low, plan, weights, potential, sheet_next, keep, give, now, then, fixed, opens):
    first, second = krylov_weights(gathered[...])
    weights[0] = jnp.broadcast_to(first, (8, LANES))
    weights[1] = jnp.broadcast_to(second, (8, LANES))
    left = info[0] == 0
    wide = low.shape[2]
    cols = wide // 2
    row = row_index(16, CHUNK)
    outside = ((info[1] == 1) & (row >= 13)) | ((info[2] == 1) & (row >= 8) & (row <= 10))
    for start in range(0, wide, CHUNK):
        part = slice(start, start + CHUNK)
        one = first * low[0, :, part] + second * low[2, :, part]
        two = first * low[1, :, part] + second * low[3, :, part]
        slide_sq = one * one + two * two
        lifted = slide_sq + speed_floor
        speed = lifted * lax.rsqrt(lifted)
        melt = melt_factor * (low[5, :, part] + low[4, :, part] * slide_sq)
        opening = speed * jnp.maximum(bump_height - plan[2, :, part], 0.0)
        opens[:, part] = opening[0:8]
        gain = melt - opening
        fixed[:, part] = plan[0, :, part] + gain
        now[:, part] = jnp.where(outside, 0.0, (plan[8, :, part] + gain) / plan[9, :, part])

    def relaxed(ref, start):
        part = slice(start, start + CHUNK)
        stop = start + CHUNK
        zero = jnp.zeros((16, LANES), F32)
        here = ref[:, part]
        east = east_of(here, ref[:, stop : stop + LANES] if stop < wide else zero)
        west = west_of(here, ref[:, start - LANES : start] if start else zero)
        burden = plan[1, :, part]
        creep = plan[2, :, part] * jnp.abs(burden - here)
        top = fixed[:, part] + creep * burden
        top += plan[3, :, part] * east + plan[4, :, part] * west
        top += plan[5, :, part] * pltpu.roll(here, 15, 0) + plan[6, :, part] * pltpu.roll(here, 1, 0)
        return top / (plan[7, :, part] + creep)

    here, there = now, then
    for _ in range(HYD_ITERS - 2):
        for start in range(0, wide, CHUNK):
            there[:, start : start + CHUNK] = jnp.where(outside, 0.0, relaxed(here, start))
        here, there = there, here
    for start in range(0, cols, CHUNK):
        sides = []
        for begin in (start, cols + start):
            part = slice(begin, begin + CHUNK)
            value = relaxed(here, begin)[0:8]
            sheet = plan[2, 0:8, part]
            pressure = plan[1, 0:8, part] - value
            potential[:, part] = value
            sheet_next[:, part] = sheet + time_step * (
                opens[:, part] - sheet * jnp.abs(pressure) * pressure
            )
            sides.append(pressure)
        part = slice(start, start + CHUNK)
        keep[:, part] = jnp.where(left, sides[0], sides[1])
        give[:, part] = jnp.where(left, sides[1], sides[0])


def velocity_kernel(weights, force, image, out, staged, done):
    layers = image.shape[1]
    first, second = weights[0, 0:1, 0:1], weights[1, 0:1, 0:1]

    def copy(layer):
        return pltpu.make_async_copy(staged.at[:, layer], out.at[:, layer], done.at[layer])

    def step(layer, carry):
        for comp in range(2):
            staged[comp, layer] = first * force[comp] + second * image[comp, layer]
        copy(layer).start()
        return carry

    lax.fori_loop(0, layers, step, 0)

    def finish(layer, carry):
        copy(layer).wait()
        return carry

    lax.fori_loop(0, layers, finish, 0)


def call(kernel, out_shape, n_in, scratch=(), smem=(), far=(), out_space=pltpu.VMEM, **kwargs):
    outs = out_shape if isinstance(out_shape, (list, tuple)) else (out_shape,)
    specs = tuple(whole(out_space) for _ in outs)
    return pl.pallas_call(
        kernel,
        out_shape=out_shape,
        in_specs=[
            whole(pltpu.SMEM if i in smem else pltpu.HBM if i in far else pltpu.VMEM) for i in range(n_in)
        ],
        out_specs=specs if isinstance(out_shape, (list, tuple)) else specs[0],
        scratch_shapes=list(scratch),
        compiler_params=pltpu.CompilerParams(vmem_limit_bytes=22 << 20),
        **kwargs,
    )


def moved(value, axis, steps):
    count = lax.axis_size(axis)
    leading, last = (max(0, -steps), min(count, count - steps))
    return lax.ppermute(value, axis, [(source, source + steps) for source in range(leading, last)])


def body(
    viscosity,
    driving_stress,
    ice_mask,
    float_mask,
    friction,
    geothermal,
    potential_prev,
    overburden,
    sheet_thick,
    channel_east,
    channel_south,
    channel_area,
):
    layers, rows, cols = viscosity.shape
    side, band = lax.axis_index("hyd"), lax.axis_index("ice")
    bands = lax.axis_size("ice")
    info = jnp.stack([side, (side == 0) & (band == 0), (side == 1) & (band == bands - 1)]).astype(jnp.int32)
    swap = [(0, 1), (1, 0)]
    fixed_inputs = (
        potential_prev,
        overburden,
        sheet_thick,
        channel_east,
        channel_south,
        channel_area,
        viscosity,
        driving_stress,
        ice_mask,
        float_mask,
        friction,
        geothermal,
    )
    placed_inputs = tuple(pltpu.with_memory_space_constraint(array, pltpu.HBM) for array in fixed_inputs)
    raw = placed_inputs[6:11]
    types = (jnp.bfloat16, F32, jnp.int32, jnp.int32, F32)

    def buffers(last):
        return [pltpu.VMEM(array.shape[:-1] + (last,), kind) for array, kind in zip(raw, types)]

    message = call(
        edge_kernel,
        shape_of(rows, LANES),
        6,
        scratch=buffers(LANES) + [pltpu.SemaphoreType.DMA((5,))],
        smem=(0,),
        far=range(1, 6),
    )(info, *raw)
    received = lax.ppermute(message, "hyd", swap)
    strip_rows, full = potential_prev.shape
    own, tile, pair, cross, fringe = call(
        strip_kernel,
        [
            shape_of(5, strip_rows, full),
            shape_of(5, rows, cols),
            shape_of(rows, full + 3 * cols + cols // 2),
            shape_of(rows, full + cols),
            shape_of(2, rows, cols),
        ],
        13,
        scratch=[
            pltpu.VMEM(array.shape[1:] if slot == 6 else array.shape, array.dtype)
            for slot, array in enumerate(fixed_inputs)
        ]
        + [pltpu.SemaphoreType.DMA((12,))],
        smem=(0,),
        far=range(1, 13),
    )(info, *placed_inputs)
    pair_in = lax.ppermute(pair, "hyd", swap)
    meet = [(2 * index + 1, 2 * index + 2) for index in range(bands - 1)]
    cross_in = lax.ppermute(cross, AXES, meet + [(high, low) for low, high in meet])
    roots, lines, force, fric, cover = call(
        root_kernel,
        [shape_of(layers, rows, cols), shape_of(3, FIELDS, cols), shape_of(2, rows, cols), shape_of(rows, cols), shape_of(rows, cols)],
        5,
        scratch=buffers(cols) + [pltpu.SemaphoreType.DMA((cols // FETCH, 5))],
        far=range(5),
    )(*raw)
    wide = cols + LANES
    block, to_south, to_north = call(
        unpack_kernel,
        [shape_of(FIELDS, rows, LANES), shape_of(FIELDS + 16, wide), shape_of(2 * FIELDS + 16, wide)],
        4,
        smem=(0,),
    )(info, received, lines, fringe)
    above = moved(to_south, "ice", 1)
    below = moved(to_north, "ice", -1)
    count = lax.axis_size("ice") * lax.axis_size("hyd")
    image, sums = call(
        operator_kernel,
        [shape_of(2, layers, rows, cols), shape_of(count, 1, LANES)],
        8,
        scratch=[
            pltpu.VMEM((8, rows, wide), F32),
            pltpu.VMEM((2, 2, rows, wide), F32),
            pltpu.VMEM((2, rows, cols), F32),
            pltpu.VMEM((2, FIELDS, cols), F32),
            pltpu.VMEM((2, rows, LANES), F32),
        ],
    )(roots, force, fric, cover, block, above, below, lines)
    gathered = lax.all_to_all(sums, AXES, 0, 0, tiled=True)
    low, plan = call(
        assemble_kernel,
        [shape_of(6, rows, full), shape_of(10, rows, full)],
        7,
        scratch=[pltpu.VMEM((5, rows, full), F32), pltpu.VMEM((5, rows, full), F32)],
        smem=(0,),
    )(info, own, tile, pair_in, cross_in, above, below)
    weights, potential, sheet_next, keep, give = call(
        hydrology_kernel,
        [
            shape_of(2, 8, LANES),
            shape_of(strip_rows, full),
            shape_of(strip_rows, full),
            shape_of(strip_rows, cols),
            shape_of(strip_rows, cols),
        ],
        4,
        scratch=[pltpu.VMEM((rows, full), F32)] * 3 + [pltpu.VMEM((strip_rows, full), F32)],
        smem=(0,),
    )(info, gathered, low, plan)
    got = lax.ppermute(give, "hyd", swap)
    velocity = pl.pallas_call(
        velocity_kernel,
        out_shape=shape_of(2, layers, rows, cols),
        in_specs=[whole(), whole(), whole()],
        out_specs=whole(pltpu.HBM),
        scratch_shapes=[pltpu.VMEM((2, layers, rows, cols), F32), pltpu.SemaphoreType.DMA((layers,))],
        compiler_params=pltpu.CompilerParams(vmem_limit_bytes=22 << 20),
    )(weights, force, pltpu.with_memory_space_constraint(image, pltpu.VMEM))

    is_left = side == 0
    effective = jnp.concatenate([jnp.where(is_left, keep, got), jnp.where(is_left, got, keep)], axis=0)
    return (velocity, effective, potential, sheet_next)


def solution(mesh):
    tiles = P("ice", "hyd")
    layered = P(None, "ice", "hyd")
    strips = P(("ice", "hyd"), None)
    return jax.shard_map(
        body,
        mesh=mesh,
        in_specs=(layered, layered, tiles, tiles, tiles, tiles) + (strips,) * 6,
        out_specs=(P(None, None, "ice", "hyd"), tiles, strips, strips),
        check_vma=False,
    )
```

```python
import functools

import jax
import jax.numpy as jnp
from jax import lax
from jax.experimental import pallas as pl
from jax.experimental.pallas import tpu as pltpu
from jax.sharding import PartitionSpec as P


HYD_ITERS = 3
vertical_weight = 4.0
relax_weight = 0.1
melt_factor = 0.5
sheet_conduct = 2.0
channel_conduct = 1.5
storage = 1.0
bump_height = 0.3
time_step = 0.5
speed_floor = 0.25

AXES = ("ice", "hyd")
F32 = jnp.float32
LANES = 128
CHUNK = 512
FETCH = 1536
FACTORS = ((4.0, 1.0), (1.0, 4.0))
FIELDS = 24
F0, FG, MASK = 20, 22, 23


def whole(space=pltpu.VMEM):
    return pl.BlockSpec(memory_space=space)


def shape_of(*dims):
    return jax.ShapeDtypeStruct(dims, F32)


def lane_index(rows, cols):
    return lax.broadcasted_iota(jnp.int32, (rows, cols), 1)


def row_index(rows, cols):
    return lax.broadcasted_iota(jnp.int32, (rows, cols), 0)


def east_of(value, right):
    cols = value.shape[1]
    joined = jnp.concatenate([value, right], axis=1)
    return pltpu.roll(joined, cols + LANES - 1, 1)[:, :cols]


def west_of(value, left):
    joined = jnp.concatenate([left, value], axis=1)
    return pltpu.roll(joined, 1, 1)[:, LANES:]


def south_of(value, below):
    rows, cols = value.shape
    return jnp.where(row_index(rows, cols) == rows - 1, below, pltpu.roll(value, rows - 1, 0))


def north_of(value, above):
    rows, cols = value.shape
    return jnp.where(row_index(rows, cols) == 0, above, pltpu.roll(value, 1, 0))


def root(weight):
    weight = weight.astype(F32)
    return weight * lax.rsqrt(weight)


def edge_kernel(half, visc, drive, mask, floating, friction, message, w, d, m, fl, fr, done):
    layers, rows, cols = visc.shape
    left_half = half[0] == 0
    start = pl.multiple_of(jnp.where(left_half, cols - LANES, 0), LANES)
    cut = pl.ds(start, LANES)
    copies = [
        pltpu.make_async_copy(source.at[..., cut], target, done.at[index])
        for index, (source, target) in enumerate(
            ((visc, w), (drive, d), (mask, m), (floating, fl), (friction, fr))
        )
    ]
    for copy in copies:
        copy.start()
    for copy in copies:
        copy.wait()
    first = jnp.where(left_half, LANES - 2, 0)
    lane = lane_index(rows, LANES)
    keep = (lane >= first) & (lane < first + 2)
    cover = m[...].astype(F32)
    fields = [root(w[layer]) * cover for layer in range(layers)]
    fields += [d[comp] * cover for comp in range(2)]
    fields += [fr[...] * (cover * (1.0 - fl[...].astype(F32))), cover]
    total = jnp.zeros((rows, LANES), F32)
    for index, field in enumerate(fields):
        part = jnp.where(keep, field, 0.0)
        total += pltpu.roll(part, 2 * index, 1) if index else part
    message[...] = total


def root_kernel(
    visc,
    drive,
    mask,
    floating,
    friction,
    geothermal,
    roots,
    lines,
    force,
    fric,
    covers,
    fringe,
    w,
    d,
    m,
    fl,
    fr,
    geo,
    done,
):
    layers, rows, cols = visc.shape
    starts = list(range(0, cols, FETCH))

    def copies(index):
        part = slice(starts[index], starts[index] + FETCH)
        return [
            pltpu.make_async_copy(source.at[..., part], target.at[..., part], done.at[index, slot])
            for slot, (source, target) in enumerate(
                ((visc, w), (drive, d), (mask, m), (floating, fl), (friction, fr), (geothermal, geo))
            )
        ]

    for index in range(len(starts)):
        for copy in copies(index):
            copy.start()
    for index, begin in enumerate(starts):
        for copy in copies(index):
            copy.wait()
        for start in range(begin, begin + FETCH, CHUNK):
            part = slice(start, start + CHUNK)
            cover = m[:, part].astype(F32)
            grounded = cover * (1.0 - fl[:, part].astype(F32))
            drag = fr[:, part] * grounded
            fric[:, part] = drag
            covers[:, part] = cover
            pushes = [d[comp, :, part] * cover for comp in range(2)]
            for comp in range(2):
                force[comp, :, part] = pushes[comp]

            def step(layer, carry, part=part, cover=cover):
                value = root(w[layer, :, part]) * cover
                roots[layer, :, part] = value
                for slot, row in enumerate((0, 1, rows - 1)):
                    lines[slot, pl.ds(layer, 1), part] = value[row : row + 1]
                return carry

            lax.fori_loop(0, layers, step, 0, unroll=2)
            for slot, row in enumerate((0, 1, rows - 1)):
                for comp in range(2):
                    lines[slot, F0 + comp : F0 + comp + 1, part] = pushes[comp][row : row + 1]
                lines[slot, FG : FG + 1, part] = drag[row : row + 1]
                lines[slot, MASK : MASK + 1, part] = cover[row : row + 1]
            fields = [roots[0, :, part], pushes[0], pushes[1], drag, geo[:, part]]
            for slot, row in enumerate((0, rows - 3)):
                parts = [placed(field, row, 3 * index) for index, field in enumerate(fields)]
                fringe[slot, :, part] = functools.reduce(jnp.add, parts)


def unpack_kernel(half, message, lines, fringe, block, to_south, to_north):
    rows = message.shape[0]
    cols = lines.shape[2]
    first = jnp.where(half[0] == 0, 0, LANES - 2)
    lane = lane_index(rows, LANES)
    keep = (lane >= first) & (lane < first + 2)
    packed = message[...]
    to_north[0:FIELDS, :cols] = lines[0]
    to_north[FIELDS : 2 * FIELDS, :cols] = lines[1]
    to_north[2 * FIELDS :, :cols] = fringe[0]
    to_south[0:FIELDS, :cols] = lines[2]
    to_south[FIELDS:, :cols] = fringe[1]
    to_north[2 * FIELDS :, cols:] = jnp.zeros((16, LANES), F32)
    to_south[FIELDS:, cols:] = jnp.zeros((16, LANES), F32)
    for index in range(FIELDS):
        part = pltpu.roll(packed, LANES - 2 * index, 1) if index else packed
        part = jnp.where(keep, part, 0.0)
        block[index] = part
        to_north[index : index + 1, cols:] = part[0:1]
        to_north[FIELDS + index : FIELDS + index + 1, cols:] = part[1:2]
        to_south[index : index + 1, cols:] = part[rows - 1 : rows]


def line_of(ref, layer, start, size):
    if size > LANES:
        return ref[pl.ds(layer, 1), start : start + size]
    return ref[pl.ds(layer, 1), start - LANES : start + size][:, LANES:]


def fold(value):
    total = None
    for row in range(0, value.shape[0], 8):
        for col in range(0, value.shape[1], LANES):
            part = value[row : row + 8, col : col + LANES]
            total = part if total is None else total + part
    return total


def relax(cover):
    return (1.0 - cover) + relax_weight * cover


def operator_kernel(
    roots, force, fric, mask, block, above, below, lines, image, sums, slopes, scaled, diag, line, edge
):
    layers, rows, cols = roots.shape
    chunks = [(start, CHUNK) for start in range(0, cols, CHUNK)]

    def columns(read_own, read_block, start, size):
        if start == cols:
            return read_block(), read_own(slice(cols - LANES, cols)), jnp.zeros((rows, LANES), F32)
        left = read_own(slice(start - LANES, start)) if start else read_block()
        stop = start + size
        right = read_own(slice(stop, stop + LANES)) if stop < cols else read_block()
        return read_own(slice(start, stop)), left, right

    squares = jnp.zeros((8, LANES), F32)
    for start, size in chunks + [(cols, LANES)]:
        part = slice(start, start + size)
        own = start < cols
        cover = mask[:, part] if own else block[MASK]
        drag = fric[:, part] if own else block[FG]
        plain = relax(cover)
        if own:
            diag[0, :, part] = plain
            diag[1, :, part] = plain + drag
        for comp, (col_factor, row_factor) in enumerate(FACTORS):
            here, left, right = columns(
                lambda cut, comp=comp: force[comp, :, cut], lambda comp=comp: block[F0 + comp], start, size
            )
            up = above[F0 + comp : F0 + comp + 1, part]
            down = below[F0 + comp : F0 + comp + 1, part]
            slopes[4 * comp, :, part] = col_factor * (here - east_of(here, right))
            slopes[4 * comp + 1, :, part] = col_factor * (here - west_of(here, left))
            slopes[4 * comp + 2, :, part] = row_factor * (here - south_of(here, down))
            slopes[4 * comp + 3, :, part] = row_factor * (here - north_of(here, up))
            scaled[0, comp, :, part] = plain * here
            scaled[1, comp, :, part] = (plain + drag) * here
            if own:
                squares += fold(here * here)

    for start, size in chunks:
        part = slice(start, start + size)
        stop = start + size
        before = slice(start - LANES, start) if start else slice(cols, cols + LANES)
        after = slice(stop, stop + LANES)
        here = below[0:layers, part]
        east = here * east_of(here, below[0:layers, after])
        west = here * west_of(here, below[0:layers, before])
        south = here * below[FIELDS : FIELDS + layers, part]
        north = here * lines[2, 0:layers, part]
        cover = below[MASK : MASK + 1, part]
        drag = jnp.where(row_index(layers, size) == 0, below[FG : FG + 1, part], 0.0)
        full = relax(cover) + drag
        for comp, (col_factor, row_factor) in enumerate(FACTORS):
            row = slice(F0 + comp, F0 + comp + 1)
            under = slice(FIELDS + F0 + comp, FIELDS + F0 + comp + 1)
            mid = below[row, part]
            line[comp, 0:layers, part] = full * mid + (
                col_factor
                * (
                    east * (mid - east_of(mid, below[row, after]))
                    + west * (mid - west_of(mid, below[row, before]))
                )
                + row_factor
                * (south * (mid - below[under, part]) + north * (mid - lines[2, row, part]))
            )

    def layer_step(layer, carry):
        kind = jnp.where(layer == 0, 1, 0)
        lower = jnp.maximum(layer - 1, 0)
        for start, size in chunks + [(cols, LANES)]:
            part = slice(start, start + size)
            here, left, right = columns(
                lambda cut: roots[layer, :, cut], lambda: block[layer], start, size
            )
            east = east_of(here, right)
            west = west_of(here, left)
            south = south_of(here, line_of(below, layer, start, size))
            north = north_of(here, line_of(above, layer, start, size))
            for comp in range(2):
                flux = (
                    east * slopes[4 * comp, :, part]
                    + west * slopes[4 * comp + 1, :, part]
                    + south * slopes[4 * comp + 2, :, part]
                    + north * slopes[4 * comp + 3, :, part]
                )
                value = scaled[kind, comp, :, part] + here * flux
                if start < cols:
                    image[comp, layer, :, part] = value
                else:
                    edge[comp] = value
        cross, square, energy = carry
        for start, size in chunks:
            part = slice(start, start + size)
            stop = start + size
            here = roots[layer, :, part]
            right = roots[layer, :, stop : stop + LANES] if stop < cols else block[layer]
            east = east_of(here, right)
            south = south_of(here, line_of(below, layer, start, size))
            beneath = roots[lower, :, part]
            to_east, to_south, to_lower, size_sq, product = 0.0, 0.0, 0.0, 0.0, 0.0
            for comp, (col_factor, row_factor) in enumerate(FACTORS):
                value = image[comp, layer, :, part]
                right = image[comp, layer, :, stop : stop + LANES] if stop < cols else edge[comp]
                step = value - east_of(value, right)
                step = step * step
                to_east += step if col_factor == 1.0 else col_factor * step
                step = value - south_of(value, line_of(line.at[comp], layer, start, size))
                step = step * step
                to_south += step if row_factor == 1.0 else row_factor * step
                step = value - image[comp, lower, :, part]
                to_lower += step * step
                size_sq += value * value
                product += value * force[comp, :, part]
            faces = here * (east * to_east + south * to_south + beneath * (vertical_weight * to_lower))
            cross += fold(product)
            square += fold(size_sq)
            energy += fold(faces + diag[kind, :, part] * size_sq)
        return cross, square, energy

    zero = jnp.zeros((8, LANES), F32)
    cross, square, energy = lax.fori_loop(0, layers, layer_step, (zero, zero, zero))
    lane = lane_index(1, LANES)
    packed = jnp.zeros((1, LANES), F32)
    for index, part in enumerate((layers * squares, cross, square, energy)):
        packed = jnp.where(lane == index, jnp.sum(part), packed)
    sums[...] = jnp.broadcast_to(packed[None], sums.shape)


def krylov_weights(gathered):
    total = jnp.sum(gathered, axis=0)
    lane = lane_index(1, LANES)

    def moment(index):
        return jnp.sum(jnp.where(lane == index, total, 0.0), axis=1, keepdims=True)

    norm, cross, square, energy = (moment(index) for index in range(4))
    step_one = norm / cross
    norm_next = step_one * (step_one * square - 2.0 * cross) + norm
    lead = 1.0 + norm_next / norm
    curve = lead * lead * cross - 2.0 * lead * step_one * square + step_one * step_one * energy
    step_two = norm_next / curve
    return step_one + step_two * lead, -step_two * step_one


def placed(value, source_row, target_row):
    rows, cols = value.shape
    moved_rows = pltpu.roll(value, (rows - source_row) % rows, 0) if source_row % rows else value
    kept = jnp.where(row_index(rows, cols) < 3, moved_rows, 0.0)
    return pltpu.roll(kept, target_row % rows, 0) if target_row % rows else kept


def strip_kernel(info, *refs):
    sources, outs = refs[:12], refs[12:16]
    own, tile, pair, cross = outs
    buffers, done = refs[16:28], refs[28]
    copies = [
        pltpu.make_async_copy(source.at[0] if slot == 6 else source, target, done.at[slot])
        for slot, (source, target) in enumerate(zip(sources, buffers))
    ]
    for copy in copies:
        copy.start()
    for copy in copies:
        copy.wait()
    prev, burden, sheet, chan_east, chan_south, area, w, d, m, fl, fr, geo = buffers
    left = info[0] == 0
    wide = prev.shape[1]
    cols = w.shape[1]
    half_cols = cols // 2
    for start in range(0, wide, CHUNK):
        part = slice(start, start + CHUNK)
        base = sheet_conduct * sheet[:, part]
        fields = [
            prev[:, part],
            burden[:, part],
            sheet[:, part],
            base + channel_conduct * chan_east[:, part].astype(F32) * area[:, part],
            base + channel_conduct * chan_south[:, part].astype(F32) * area[:, part],
        ]
        first, last = None, None
        for index, field in enumerate(fields):
            own[index, :, part] = field
            both = jnp.concatenate([field, field], axis=0)
            head, tail = placed(both, 0, 3 * index), placed(both, 5, 3 * index)
            first = head if first is None else first + head
            last = tail if last is None else last + tail
        pair[:, part] = jnp.where(left, last, first)
        cross[:, part] = jnp.where(left, first, last)
    for start in range(0, cols, CHUNK):
        part = slice(start, start + CHUNK)

        def shifted_part(offset, start=start):
            return slice(wide + offset + start, wide + offset + start + CHUNK)

        cover = m[:, part].astype(F32)
        fields = [
            root(w[:, part]) * cover,
            d[0, :, part] * cover,
            d[1, :, part] * cover,
            fr[:, part] * (cover * (1.0 - fl[:, part].astype(F32))),
            geo[:, part],
        ]
        first, last, middle, halves = None, None, None, []
        for index, field in enumerate(fields):
            tile[index, :, part] = field
            head, tail = placed(field, 0, 3 * index), placed(field, 13, 3 * index)
            inner = jnp.where(left, placed(field, 5, 3 * index), placed(field, 8, 3 * index))
            first = head if first is None else first + head
            last = tail if last is None else last + tail
            middle = inner if middle is None else middle + inner
            halves.append(jnp.where(left, field[8:16], field[0:8]))
        cross[:, shifted_part(0)] = jnp.where(left, first, last)
        pair[:, shifted_part(0)] = jnp.concatenate(halves[0:2], axis=0)
        pair[:, shifted_part(cols)] = jnp.concatenate(halves[2:4], axis=0)
        pair[:, shifted_part(2 * cols)] = middle
        row = 0 if start < half_cols else 8
        place = wide + 3 * cols + start % half_cols
        pair[row : row + 8, place : place + CHUNK] = halves[4]


def assemble_kernel(info, own, tile, pair, cross, above, below, low, plan, base, hyd):
    left = info[0] == 0
    wide = own.shape[2]
    cols = tile.shape[2]
    half_cols = cols // 2
    row = row_index(16, CHUNK)
    in_north = row >= 13
    in_south = (row >= 8) & (row <= 10)
    blank = jnp.zeros((8, CHUNK), F32)

    def circle(main, index, mine, theirs):
        north = jnp.where(left, theirs, mine)
        south = jnp.where(left, mine, theirs)
        north = pltpu.roll(north, (13 - 3 * index) % 16, 0)
        south = pltpu.roll(south, (8 - 3 * index) % 16, 0)
        both = jnp.concatenate([main, blank], axis=0)
        return jnp.where(in_north, north, jnp.where(in_south, south, both))

    for start in range(0, wide, CHUNK):
        part = slice(start, start + CHUNK)
        from_pair, from_cross = pair[:, part], cross[:, part]
        for index in range(5):
            hyd[index, :, part] = circle(own[index, :, part], index, from_pair, from_cross)
    for start in range(0, cols, CHUNK):
        part = slice(start, start + CHUNK)
        middle = pair[:, wide + 2 * cols + start : wide + 2 * cols + start + CHUNK]
        outer = cross[:, wide + start : wide + start + CHUNK]
        beyond = jnp.where(
            left, above[FIELDS : FIELDS + 16, part], below[2 * FIELDS : 2 * FIELDS + 16, part]
        )
        replaced = (left & in_north) | (jnp.logical_not(left) & in_south)
        for index in range(5):
            field = tile[index, :, part]
            swapped = jnp.concatenate([field[8:16], field[0:8]], axis=0)
            here = jnp.where(left, field, swapped)
            far = jnp.where(
                left,
                pltpu.roll(beyond, (13 - 3 * index) % 16, 0),
                pltpu.roll(beyond, (8 - 3 * index) % 16, 0),
            )
            here = jnp.where(replaced, far, here)
            if index < 4:
                place = wide + (index // 2) * cols + start
                top = (index % 2) * 8
            else:
                place = wide + 3 * cols + start % half_cols
                top = 0 if start < half_cols else 8
            there = circle(pair[top : top + 8, place : place + CHUNK], index, middle, outer)
            base[index, :, part] = jnp.where(left, here, there)
            base[index, :, cols + start : cols + start + CHUNK] = jnp.where(left, there, here)

    def neighbours(ref, start):
        stop = start + CHUNK
        zero = jnp.zeros((16, LANES), F32)
        here = ref[:, start:stop]
        right = ref[:, stop : stop + LANES] if stop < wide else zero
        leftward = ref[:, start - LANES : start] if start else zero
        return here, east_of(here, right), west_of(here, leftward), pltpu.roll(here, 15, 0), pltpu.roll(here, 1, 0)

    for start in range(0, wide, CHUNK):
        part = slice(start, start + CHUNK)
        here, east, west, south, north = neighbours(base.at[0], start)
        drag = base[3, :, part]
        diagonal = relax(jnp.where(here > 0.0, 1.0, 0.0)) + drag
        for comp, (col_factor, row_factor) in enumerate(FACTORS):
            mid, mid_e, mid_w, mid_s, mid_n = neighbours(base.at[1 + comp], start)
            low[comp, :, part] = mid
            low[2 + comp, :, part] = diagonal * mid + here * (
                col_factor * (east * (mid - mid_e) + west * (mid - mid_w))
                + row_factor * (south * (mid - mid_s) + north * (mid - mid_n))
            )
        low[4, :, part] = drag
        low[5, :, part] = base[4, :, part]
        prev, prev_e, prev_w, prev_s, prev_n = neighbours(hyd.at[0], start)
        burden, sheet = hyd[1, :, part], hyd[2, :, part]
        to_east, _, to_west, _, _ = neighbours(hyd.at[3], start)
        to_south = hyd[4, :, part]
        to_north = pltpu.roll(to_south, 1, 0)
        total = storage + (to_east + to_west + to_south + to_north)
        creep = sheet * jnp.abs(burden - prev)
        known = storage * prev + creep * burden
        known += to_east * prev_e + to_west * prev_w + to_south * prev_s + to_north * prev_n
        for index, value in enumerate(
            (storage * prev, burden, sheet, to_east, to_west, to_south, to_north, total, known, total + creep)
        ):
            plan[index, :, part] = value


def weights_kernel(gathered, weights):
    first, second = krylov_weights(gathered[...])
    weights[0] = jnp.broadcast_to(first, (8, LANES))
    weights[1] = jnp.broadcast_to(second, (8, LANES))


def hydrology_kernel(info, weights, low, plan, potential, sheet_next, keep, give, now, then, fixed, opens):
    first, second = weights[0, 0:1, 0:1], weights[1, 0:1, 0:1]
    left = info[0] == 0
    wide = low.shape[2]
    cols = wide // 2
    row = row_index(16, CHUNK)
    outside = ((info[1] == 1) & (row >= 13)) | ((info[2] == 1) & (row >= 8) & (row <= 10))
    for start in range(0, wide, CHUNK):
        part = slice(start, start + CHUNK)
        one = first * low[0, :, part] + second * low[2, :, part]
        two = first * low[1, :, part] + second * low[3, :, part]
        slide_sq = one * one + two * two
        lifted = slide_sq + speed_floor
        speed = lifted * lax.rsqrt(lifted)
        melt = melt_factor * (low[5, :, part] + low[4, :, part] * slide_sq)
        opening = speed * jnp.maximum(bump_height - plan[2, :, part], 0.0)
        opens[:, part] = opening[0:8]
        gain = melt - opening
        fixed[:, part] = plan[0, :, part] + gain
        now[:, part] = jnp.where(outside, 0.0, (plan[8, :, part] + gain) / plan[9, :, part])

    def relaxed(ref, start):
        part = slice(start, start + CHUNK)
        stop = start + CHUNK
        zero = jnp.zeros((16, LANES), F32)
        here = ref[:, part]
        east = east_of(here, ref[:, stop : stop + LANES] if stop < wide else zero)
        west = west_of(here, ref[:, start - LANES : start] if start else zero)
        burden = plan[1, :, part]
        creep = plan[2, :, part] * jnp.abs(burden - here)
        top = fixed[:, part] + creep * burden
        top += plan[3, :, part] * east + plan[4, :, part] * west
        top += plan[5, :, part] * pltpu.roll(here, 15, 0) + plan[6, :, part] * pltpu.roll(here, 1, 0)
        return top / (plan[7, :, part] + creep)

    here, there = now, then
    for _ in range(HYD_ITERS - 2):
        for start in range(0, wide, CHUNK):
            there[:, start : start + CHUNK] = jnp.where(outside, 0.0, relaxed(here, start))
        here, there = there, here
    for start in range(0, cols, CHUNK):
        sides = []
        for begin in (start, cols + start):
            part = slice(begin, begin + CHUNK)
            value = relaxed(here, begin)[0:8]
            sheet = plan[2, 0:8, part]
            pressure = plan[1, 0:8, part] - value
            potential[:, part] = value
            sheet_next[:, part] = sheet + time_step * (
                opens[:, part] - sheet * jnp.abs(pressure) * pressure
            )
            sides.append(pressure)
        part = slice(start, start + CHUNK)
        keep[:, part] = jnp.where(left, sides[0], sides[1])
        give[:, part] = jnp.where(left, sides[1], sides[0])


def velocity_kernel(weights, force, image, out, staged, done):
    layers = image.shape[1]
    first, second = weights[0, 0:1, 0:1], weights[1, 0:1, 0:1]

    def copy(layer):
        return pltpu.make_async_copy(staged.at[:, layer], out.at[:, layer], done.at[layer])

    def step(layer, carry):
        for comp in range(2):
            staged[comp, layer] = first * force[comp] + second * image[comp, layer]
        copy(layer).start()
        return carry

    lax.fori_loop(0, layers, step, 0)

    def finish(layer, carry):
        copy(layer).wait()
        return carry

    lax.fori_loop(0, layers, finish, 0)


def call(kernel, out_shape, n_in, scratch=(), smem=(), far=(), out_space=pltpu.VMEM, **kwargs):
    outs = out_shape if isinstance(out_shape, (list, tuple)) else (out_shape,)
    specs = tuple(whole(out_space) for _ in outs)
    return pl.pallas_call(
        kernel,
        out_shape=out_shape,
        in_specs=[
            whole(pltpu.SMEM if i in smem else pltpu.HBM if i in far else pltpu.VMEM) for i in range(n_in)
        ],
        out_specs=specs if isinstance(out_shape, (list, tuple)) else specs[0],
        scratch_shapes=list(scratch),
        compiler_params=pltpu.CompilerParams(vmem_limit_bytes=22 << 20),
        **kwargs,
    )


def moved(value, axis, steps):
    count = lax.axis_size(axis)
    leading, last = (max(0, -steps), min(count, count - steps))
    return lax.ppermute(value, axis, [(source, source + steps) for source in range(leading, last)])


def body(
    viscosity,
    driving_stress,
    ice_mask,
    float_mask,
    friction,
    geothermal,
    potential_prev,
    overburden,
    sheet_thick,
    channel_east,
    channel_south,
    channel_area,
):
    layers, rows, cols = viscosity.shape
    side, band = lax.axis_index("hyd"), lax.axis_index("ice")
    bands = lax.axis_size("ice")
    info = jnp.stack([side, (side == 0) & (band == 0), (side == 1) & (band == bands - 1)]).astype(jnp.int32)
    swap = [(0, 1), (1, 0)]
    fixed_inputs = (
        potential_prev,
        overburden,
        sheet_thick,
        channel_east,
        channel_south,
        channel_area,
        viscosity,
        driving_stress,
        ice_mask,
        float_mask,
        friction,
        geothermal,
    )
    placed_inputs = tuple(pltpu.with_memory_space_constraint(array, pltpu.HBM) for array in fixed_inputs)
    raw = placed_inputs[6:11]
    types = (jnp.bfloat16, F32, jnp.int32, jnp.int32, F32)

    def buffers(last):
        return [pltpu.VMEM(array.shape[:-1] + (last,), kind) for array, kind in zip(raw, types)]

    message = call(
        edge_kernel,
        shape_of(rows, LANES),
        6,
        scratch=buffers(LANES) + [pltpu.SemaphoreType.DMA((5,))],
        smem=(0,),
        far=range(1, 6),
    )(info, *raw)
    received = lax.ppermute(message, "hyd", swap)
    roots, lines, force, fric, cover, fringe = call(
        root_kernel,
        [shape_of(layers, rows, cols), shape_of(3, FIELDS, cols), shape_of(2, rows, cols), shape_of(rows, cols), shape_of(rows, cols), shape_of(2, rows, cols)],
        6,
        scratch=buffers(cols) + [pltpu.VMEM((rows, cols), F32), pltpu.SemaphoreType.DMA((cols // FETCH, 6))],
        far=range(6),
    )(*placed_inputs[6:])
    wide = cols + LANES
    block, to_south, to_north = call(
        unpack_kernel,
        [shape_of(FIELDS, rows, LANES), shape_of(FIELDS + 16, wide), shape_of(2 * FIELDS + 16, wide)],
        4,
        smem=(0,),
    )(info, received, lines, fringe)
    to_south, to_north, late = lax.optimization_barrier((to_south, to_north, info))
    above = moved(to_south, "ice", 1)
    below = moved(to_north, "ice", -1)
    strip_rows, full = potential_prev.shape
    own, tile, pair, cross = call(
        strip_kernel,
        [
            shape_of(5, strip_rows, full),
            shape_of(5, rows, cols),
            shape_of(rows, full + 3 * cols + cols // 2),
            shape_of(rows, full + cols),
        ],
        13,
        scratch=[
            pltpu.VMEM(array.shape[1:] if slot == 6 else array.shape, array.dtype)
            for slot, array in enumerate(fixed_inputs)
        ]
        + [pltpu.SemaphoreType.DMA((12,))],
        smem=(0,),
        far=range(1, 13),
    )(late, *placed_inputs)
    pair_in = lax.ppermute(pair, "hyd", swap)
    meet = [(2 * index + 1, 2 * index + 2) for index in range(bands - 1)]
    cross_in = lax.ppermute(cross, AXES, meet + [(high, low) for low, high in meet])
    count = lax.axis_size("ice") * lax.axis_size("hyd")
    image, sums = call(
        operator_kernel,
        [shape_of(2, layers, rows, cols), shape_of(count, 1, LANES)],
        8,
        scratch=[
            pltpu.VMEM((8, rows, wide), F32),
            pltpu.VMEM((2, 2, rows, wide), F32),
            pltpu.VMEM((2, rows, cols), F32),
            pltpu.VMEM((2, FIELDS, cols), F32),
            pltpu.VMEM((2, rows, LANES), F32),
        ],
    )(roots, force, fric, cover, block, above, below, lines)
    gathered = lax.all_to_all(sums, AXES, 0, 0, tiled=True)
    weights = call(weights_kernel, shape_of(2, 8, LANES), 1)(gathered)
    low, plan = call(
        assemble_kernel,
        [shape_of(6, rows, full), shape_of(10, rows, full)],
        7,
        scratch=[pltpu.VMEM((5, rows, full), F32), pltpu.VMEM((5, rows, full), F32)],
        smem=(0,),
    )(info, own, tile, pair_in, cross_in, above, below)
    potential, sheet_next, keep, give = call(
        hydrology_kernel,
        [
            shape_of(strip_rows, full),
            shape_of(strip_rows, full),
            shape_of(strip_rows, cols),
            shape_of(strip_rows, cols),
        ],
        4,
        scratch=[pltpu.VMEM((rows, full), F32)] * 3 + [pltpu.VMEM((strip_rows, full), F32)],
        smem=(0,),
    )(info, weights, low, plan)
    got = lax.ppermute(give, "hyd", swap)
    velocity = pl.pallas_call(
        velocity_kernel,
        out_shape=shape_of(2, layers, rows, cols),
        in_specs=[whole(), whole(), whole()],
        out_specs=whole(pltpu.HBM),
        scratch_shapes=[pltpu.VMEM((2, layers, rows, cols), F32), pltpu.SemaphoreType.DMA((layers,))],
        compiler_params=pltpu.CompilerParams(vmem_limit_bytes=22 << 20),
    )(weights, force, pltpu.with_memory_space_constraint(image, pltpu.VMEM))

    is_left = side == 0
    effective = jnp.concatenate([jnp.where(is_left, keep, got), jnp.where(is_left, got, keep)], axis=0)
    return (velocity, effective, potential, sheet_next)


def solution(mesh):
    tiles = P("ice", "hyd")
    layered = P(None, "ice", "hyd")
    strips = P(("ice", "hyd"), None)

    return jax.shard_map(
        body,
        mesh=mesh,
        in_specs=(layered, layered, tiles, tiles, tiles, tiles) + (strips,) * 6,
        out_specs=(P(None, None, "ice", "hyd"), tiles, strips, strips),
        check_vma=False,
    )
```

```python
import functools

import jax
import jax.numpy as jnp
from jax import lax
from jax.experimental import pallas as pl
from jax.experimental.pallas import tpu as pltpu
from jax.sharding import PartitionSpec as P


HYD_ITERS = 3
relax_weight = 0.1
melt_factor = 0.5
sheet_conduct = 2.0
channel_conduct = 1.5
storage = 1.0
bump_height = 0.3
time_step = 0.5
speed_floor = 0.25

AXES = ("ice", "hyd")
F32 = jnp.float32
LANES = 128
CHUNK = 512
FETCH = 1536
FACTORS = ((4.0, 1.0), (1.0, 4.0))
FIELDS = 24
F0, FG, MASK = 20, 22, 23


def whole(space=pltpu.VMEM):
    return pl.BlockSpec(memory_space=space)


def shape_of(*dims):
    return jax.ShapeDtypeStruct(dims, F32)


def lane_index(rows, cols):
    return lax.broadcasted_iota(jnp.int32, (rows, cols), 1)


def row_index(rows, cols):
    return lax.broadcasted_iota(jnp.int32, (rows, cols), 0)


def east_of(value, right):
    cols = value.shape[1]
    joined = jnp.concatenate([value, right], axis=1)
    return pltpu.roll(joined, cols + LANES - 1, 1)[:, :cols]


def west_of(value, left):
    joined = jnp.concatenate([left, value], axis=1)
    return pltpu.roll(joined, 1, 1)[:, LANES:]


def root(weight):
    weight = weight.astype(F32)
    return weight * lax.rsqrt(weight)


def edge_kernel(half, visc, drive, mask, floating, friction, message, w, d, m, fl, fr, done):
    layers, rows, cols = visc.shape
    left_half = half[0] == 0
    start = pl.multiple_of(jnp.where(left_half, cols - LANES, 0), LANES)
    cut = pl.ds(start, LANES)
    copies = [
        pltpu.make_async_copy(source.at[..., cut], target, done.at[index])
        for index, (source, target) in enumerate(
            ((visc, w), (drive, d), (mask, m), (floating, fl), (friction, fr))
        )
    ]
    for copy in copies:
        copy.start()
    for copy in copies:
        copy.wait()
    first = jnp.where(left_half, LANES - 2, 0)
    lane = lane_index(rows, LANES)
    keep = (lane >= first) & (lane < first + 2)
    cover = m[...].astype(F32)
    fields = [root(w[layer]) * cover for layer in range(layers)]
    fields += [d[comp] * cover for comp in range(2)]
    fields += [fr[...] * (cover * (1.0 - fl[...].astype(F32))), cover]
    total = jnp.zeros((rows, LANES), F32)
    for index, field in enumerate(fields):
        part = jnp.where(keep, field, 0.0)
        total += pltpu.roll(part, 2 * index, 1) if index else part
    message[...] = total


def root_kernel(
    visc,
    drive,
    mask,
    floating,
    friction,
    geothermal,
    roots,
    lines,
    force,
    fric,
    covers,
    fringe,
    w,
    d,
    m,
    fl,
    fr,
    geo,
    done,
):
    layers, rows, cols = visc.shape
    starts = list(range(0, cols, FETCH))

    def copies(index):
        part = slice(starts[index], starts[index] + FETCH)
        return [
            pltpu.make_async_copy(source.at[..., part], target.at[..., part], done.at[index, slot])
            for slot, (source, target) in enumerate(
                ((visc, w), (drive, d), (mask, m), (floating, fl), (friction, fr), (geothermal, geo))
            )
        ]

    for index in range(len(starts)):
        for copy in copies(index):
            copy.start()
    for index, begin in enumerate(starts):
        for copy in copies(index):
            copy.wait()
        for start in range(begin, begin + FETCH, CHUNK):
            part = slice(start, start + CHUNK)
            cover = m[:, part].astype(F32)
            grounded = cover * (1.0 - fl[:, part].astype(F32))
            drag = fr[:, part] * grounded
            fric[:, part] = drag
            covers[:, part] = cover
            pushes = [d[comp, :, part] * cover for comp in range(2)]
            for comp in range(2):
                force[comp, :, part] = pushes[comp]

            def step(layer, carry, part=part, cover=cover):
                value = root(w[layer, :, part]) * cover
                roots[layer, :, part] = value
                for slot, row in enumerate((0, 1, rows - 1)):
                    lines[slot, pl.ds(layer, 1), part] = value[row : row + 1]
                return carry

            lax.fori_loop(0, layers, step, 0, unroll=2)
            for slot, row in enumerate((0, 1, rows - 1)):
                for comp in range(2):
                    lines[slot, F0 + comp : F0 + comp + 1, part] = pushes[comp][row : row + 1]
                lines[slot, FG : FG + 1, part] = drag[row : row + 1]
                lines[slot, MASK : MASK + 1, part] = cover[row : row + 1]
            fields = [roots[0, :, part], pushes[0], pushes[1], drag, geo[:, part]]
            for slot, row in enumerate((0, rows - 3)):
                parts = [placed(field, row, 3 * index) for index, field in enumerate(fields)]
                fringe[slot, :, part] = functools.reduce(jnp.add, parts)


def unpack_kernel(half, message, lines, fringe, block, to_south, to_north):
    rows = message.shape[0]
    cols = lines.shape[2]
    first = jnp.where(half[0] == 0, 0, LANES - 2)
    lane = lane_index(rows, LANES)
    keep = (lane >= first) & (lane < first + 2)
    packed = message[...]
    to_north[0:FIELDS, :cols] = lines[0]
    to_north[FIELDS : 2 * FIELDS, :cols] = lines[1]
    to_north[2 * FIELDS :, :cols] = fringe[0]
    to_south[0:FIELDS, :cols] = lines[2]
    to_south[FIELDS:, :cols] = fringe[1]
    to_north[2 * FIELDS :, cols:] = jnp.zeros((16, LANES), F32)
    to_south[FIELDS:, cols:] = jnp.zeros((16, LANES), F32)
    for index in range(FIELDS):
        part = pltpu.roll(packed, LANES - 2 * index, 1) if index else packed
        part = jnp.where(keep, part, 0.0)
        block[index] = part
        to_north[index : index + 1, cols:] = part[0:1]
        to_north[FIELDS + index : FIELDS + index + 1, cols:] = part[1:2]
        to_south[index : index + 1, cols:] = part[rows - 1 : rows]


def line_of(ref, layer, start, size):
    if size > LANES:
        return ref[pl.ds(layer, 1), start : start + size]
    return ref[pl.ds(layer, 1), start - LANES : start + size][:, LANES:]


def fold(value):
    total = None
    for row in range(0, value.shape[0], 8):
        for col in range(0, value.shape[1], LANES):
            part = value[row : row + 8, col : col + LANES]
            total = part if total is None else total + part
    return total


def relax(cover):
    return (1.0 - cover) + relax_weight * cover


def south_rows(value, below):
    upper, lower = value[0:8], value[8:16]
    last = row_index(8, value.shape[1]) == 7
    next_row = pltpu.roll(lower, 7, 0)
    return jnp.concatenate(
        [jnp.where(last, next_row, pltpu.roll(upper, 7, 0)), jnp.where(last, below, next_row)], axis=0
    )


def north_rows(value, above):
    upper, lower = value[0:8], value[8:16]
    first = row_index(8, value.shape[1]) == 0
    previous = pltpu.roll(upper, 1, 0)
    return jnp.concatenate(
        [jnp.where(first, above, previous), jnp.where(first, previous, pltpu.roll(lower, 1, 0))], axis=0
    )


def columns(read_own, read_block, start, size, cols, rows):
    if start == cols:
        return read_block(), read_own(slice(cols - LANES, cols)), jnp.zeros((rows, LANES), F32)
    left = read_own(slice(start - LANES, start)) if start else read_block()
    stop = start + size
    right = read_own(slice(stop, stop + LANES)) if stop < cols else read_block()
    return read_own(slice(start, stop)), left, right


def image_kernel(roots, force, fric, mask, block, image, to_east, to_south, slopes, scaled):
    layers, rows, cols = roots.shape
    chunks = [(start, CHUNK) for start in range(0, cols, CHUNK)]
    for start, size in chunks:
        part = slice(start, start + size)
        nothing = jnp.zeros((1, size), F32)
        plain = relax(mask[:, part])
        for comp, (col_factor, row_factor) in enumerate(FACTORS):
            here, left, right = columns(
                lambda cut, comp=comp: force[comp, :, cut],
                lambda comp=comp: block[F0 + comp],
                start,
                size,
                cols,
                rows,
            )
            slopes[4 * comp, :, part] = col_factor * (here - east_of(here, right))
            slopes[4 * comp + 1, :, part] = col_factor * (here - west_of(here, left))
            slopes[4 * comp + 2, :, part] = row_factor * (here - south_rows(here, nothing))
            slopes[4 * comp + 3, :, part] = row_factor * (here - north_rows(here, nothing))
            scaled[0, comp, :, part] = plain * here
            scaled[1, comp, :, part] = (plain + fric[:, part]) * here

    def layer_step(layer, carry):
        kind = jnp.where(layer == 0, 1, 0)
        for start, size in chunks:
            part = slice(start, start + size)
            nothing = jnp.zeros((1, size), F32)
            here, left, right = columns(
                lambda cut: roots[layer, :, cut], lambda: block[layer], start, size, cols, rows
            )
            east = here * east_of(here, right)
            west = here * west_of(here, left)
            south = here * south_rows(here, nothing)
            north = north_rows(south, nothing)
            to_east[layer, :, part] = east
            to_south[layer, :, part] = south
            for comp in range(2):
                image[comp, layer, :, part] = scaled[kind, comp, :, part] + (
                    east * slopes[4 * comp, :, part]
                    + west * slopes[4 * comp + 1, :, part]
                    + south * slopes[4 * comp + 2, :, part]
                    + north * slopes[4 * comp + 3, :, part]
                )
        return carry

    lax.fori_loop(0, layers, layer_step, 0)


def moment_kernel(
    roots,
    force,
    fric,
    mask,
    block,
    above,
    below,
    lines,
    started,
    to_east,
    faces_before,
    image,
    faces,
    sums,
    line,
    edge,
    repair,
    outer,
    totals,
):
    layers, rows, cols = roots.shape
    chunks = [(start, CHUNK) for start in range(0, cols, CHUNK)]
    block_part = slice(cols, cols + LANES)

    for start, size in chunks:
        part = slice(start, start + size)
        stop = start + size
        before = slice(start - LANES, start) if start else block_part
        after = slice(stop, stop + LANES)
        here = below[0:layers, part]
        top = lines[0, 0:layers, part] * above[0:layers, part]
        north = here * lines[2, 0:layers, part]
        outer[0:layers, part] = north
        east = here * east_of(here, below[0:layers, after])
        west = here * west_of(here, below[0:layers, before])
        south = here * below[FIELDS : FIELDS + layers, part]
        drag = jnp.where(row_index(layers, size) == 0, below[FG : FG + 1, part], 0.0)
        full = relax(below[MASK : MASK + 1, part]) + drag
        for comp, (col_factor, row_factor) in enumerate(FACTORS):
            row = slice(F0 + comp, F0 + comp + 1)
            under = slice(FIELDS + F0 + comp, FIELDS + F0 + comp + 1)
            mid = below[row, part]
            rise = row_factor * (mid - lines[2, row, part])
            repair[comp, 0:layers, part] = top * (row_factor * (lines[0, row, part] - above[row, part]))
            repair[2 + comp, 0:layers, part] = north * (-rise)
            line[comp, 0:layers, part] = full * mid + (
                col_factor
                * (
                    east * (mid - east_of(mid, below[row, after]))
                    + west * (mid - west_of(mid, below[row, before]))
                )
                + (row_factor * south * (mid - below[under, part]) + north * rise)
            )
        for index in range(3):
            totals[index, :, part] = jnp.zeros((rows, size), F32)

    nothing = jnp.zeros((rows, LANES), F32)
    side_slopes = []
    for comp, (col_factor, row_factor) in enumerate(FACTORS):
        here = block[F0 + comp]
        left = force[comp, :, cols - LANES : cols]
        up = above[F0 + comp : F0 + comp + 1, block_part]
        down = below[F0 + comp : F0 + comp + 1, block_part]
        side_slopes.append(
            (
                col_factor * (here - east_of(here, nothing)),
                col_factor * (here - west_of(here, left)),
                row_factor * (here - south_rows(here, down)),
                row_factor * (here - north_rows(here, up)),
            )
        )
    side_plain = relax(block[MASK])

    def layer_step(layer, carry):
        lower = jnp.maximum(layer - 1, 0)
        here = block[layer]
        east = here * east_of(here, nothing)
        west = here * west_of(here, roots[layer, :, cols - LANES : cols])
        south = here * south_rows(here, line_of(below, layer, cols, LANES))
        north = here * north_rows(here, line_of(above, layer, cols, LANES))
        full = side_plain + jnp.where(layer == 0, 1.0, 0.0) * block[FG]
        for comp in range(2):
            slope = side_slopes[comp]
            edge[comp] = full * block[F0 + comp] + (
                (east * slope[0] + west * slope[1]) + (south * slope[2] + north * slope[3])
            )
        for start, size in chunks:
            part = slice(start, start + size)
            faces[layer, rows - 1 : rows, part] = outer[pl.ds(layer, 1), part]
            for comp in range(2):
                image[comp, layer, 0:1, part] = (
                    image[comp, layer, 0:1, part] + repair[comp, pl.ds(layer, 1), part]
                )
                image[comp, layer, rows - 1 : rows, part] = (
                    image[comp, layer, rows - 1 : rows, part] + repair[2 + comp, pl.ds(layer, 1), part]
                )
        quads, singles = carry
        for start, size in chunks:
            part = slice(start, start + size)
            stop = start + size
            east = to_east[layer, :, part]
            south = faces[layer, :, part]
            down = roots[layer, :, part] * roots[lower, :, part]
            squares, falls = [], []
            lows, length = None, None
            for comp in range(2):
                value = image[comp, layer, :, part]
                right = image[comp, layer, :, stop : stop + LANES] if stop < cols else edge[comp]
                step = value - east_of(value, right)
                squares.append(step * step)
                step = value - south_rows(value, line[comp, pl.ds(layer, 1), part])
                falls.append(step * step)
                step = value - image[comp, lower, :, part]
                lows = step * step if lows is None else lows + step * step
                length = value * value if length is None else length + value * value
                totals[comp, :, part] += value
            totals[2, :, part] += length
            quads += fold(east * squares[0] + south * falls[1] + down * lows)
            singles += fold(east * squares[1] + south * falls[0])
        return quads, singles

    zero = jnp.zeros((8, LANES), F32)
    quads, singles = lax.fori_loop(0, layers, layer_step, (zero, zero))
    norm, cross, square, energy = zero, zero, zero, 4.0 * quads + singles
    for start, size in chunks:
        part = slice(start, start + size)
        one, two = force[0, :, part], force[1, :, part]
        norm += fold(one * one + two * two)
        cross += fold(one * totals[0, :, part] + two * totals[1, :, part])
        length = totals[2, :, part]
        square += fold(length)
        one, two = image[0, 0, :, part], image[1, 0, :, part]
        energy += fold(relax(mask[:, part]) * length + fric[:, part] * (one * one + two * two))
    lane = lane_index(1, LANES)
    packed = jnp.zeros((1, LANES), F32)
    for index, part in enumerate((layers * norm, cross, square, energy)):
        packed = jnp.where(lane == index, jnp.sum(part), packed)
    sums[...] = jnp.broadcast_to(packed[None], sums.shape)


def krylov_weights(gathered):
    total = jnp.sum(gathered, axis=0)
    lane = lane_index(1, LANES)

    def moment(index):
        return jnp.sum(jnp.where(lane == index, total, 0.0), axis=1, keepdims=True)

    norm, cross, square, energy = (moment(index) for index in range(4))
    step_one = norm / cross
    norm_next = step_one * (step_one * square - 2.0 * cross) + norm
    lead = 1.0 + norm_next / norm
    curve = lead * lead * cross - 2.0 * lead * step_one * square + step_one * step_one * energy
    step_two = norm_next / curve
    return step_one + step_two * lead, -step_two * step_one


def placed(value, source_row, target_row):
    rows, cols = value.shape
    moved_rows = pltpu.roll(value, (rows - source_row) % rows, 0) if source_row % rows else value
    kept = jnp.where(row_index(rows, cols) < 3, moved_rows, 0.0)
    return pltpu.roll(kept, target_row % rows, 0) if target_row % rows else kept


def strip_kernel(info, *refs):
    sources, outs = refs[:12], refs[12:16]
    own, tile, pair, cross = outs
    buffers, done = refs[16:28], refs[28]
    copies = [
        pltpu.make_async_copy(source.at[0] if slot == 6 else source, target, done.at[slot])
        for slot, (source, target) in enumerate(zip(sources, buffers))
    ]
    for copy in copies:
        copy.start()
    for copy in copies:
        copy.wait()
    prev, burden, sheet, chan_east, chan_south, area, w, d, m, fl, fr, geo = buffers
    left = info[0] == 0
    wide = prev.shape[1]
    cols = w.shape[1]
    half_cols = cols // 2
    for start in range(0, wide, CHUNK):
        part = slice(start, start + CHUNK)
        base = sheet_conduct * sheet[:, part]
        fields = [
            prev[:, part],
            burden[:, part],
            sheet[:, part],
            base + channel_conduct * chan_east[:, part].astype(F32) * area[:, part],
            base + channel_conduct * chan_south[:, part].astype(F32) * area[:, part],
        ]
        first, last = None, None
        for index, field in enumerate(fields):
            own[index, :, part] = field
            both = jnp.concatenate([field, field], axis=0)
            head, tail = placed(both, 0, 3 * index), placed(both, 5, 3 * index)
            first = head if first is None else first + head
            last = tail if last is None else last + tail
        pair[:, part] = jnp.where(left, last, first)
        cross[:, part] = jnp.where(left, first, last)
    for start in range(0, cols, CHUNK):
        part = slice(start, start + CHUNK)

        def shifted_part(offset, start=start):
            return slice(wide + offset + start, wide + offset + start + CHUNK)

        cover = m[:, part].astype(F32)
        fields = [
            root(w[:, part]) * cover,
            d[0, :, part] * cover,
            d[1, :, part] * cover,
            fr[:, part] * (cover * (1.0 - fl[:, part].astype(F32))),
            geo[:, part],
        ]
        first, last, middle, halves = None, None, None, []
        for index, field in enumerate(fields):
            tile[index, :, part] = field
            head, tail = placed(field, 0, 3 * index), placed(field, 13, 3 * index)
            inner = jnp.where(left, placed(field, 5, 3 * index), placed(field, 8, 3 * index))
            first = head if first is None else first + head
            last = tail if last is None else last + tail
            middle = inner if middle is None else middle + inner
            halves.append(jnp.where(left, field[8:16], field[0:8]))
        cross[:, shifted_part(0)] = jnp.where(left, first, last)
        pair[:, shifted_part(0)] = jnp.concatenate(halves[0:2], axis=0)
        pair[:, shifted_part(cols)] = jnp.concatenate(halves[2:4], axis=0)
        pair[:, shifted_part(2 * cols)] = middle
        row = 0 if start < half_cols else 8
        place = wide + 3 * cols + start % half_cols
        pair[row : row + 8, place : place + CHUNK] = halves[4]


def assemble_kernel(info, own, tile, pair, cross, above, below, low, plan, base, hyd):
    left = info[0] == 0
    wide = own.shape[2]
    cols = tile.shape[2]
    half_cols = cols // 2
    row = row_index(16, CHUNK)
    in_north = row >= 13
    in_south = (row >= 8) & (row <= 10)
    blank = jnp.zeros((8, CHUNK), F32)

    def circle(main, index, mine, theirs):
        north = jnp.where(left, theirs, mine)
        south = jnp.where(left, mine, theirs)
        north = pltpu.roll(north, (13 - 3 * index) % 16, 0)
        south = pltpu.roll(south, (8 - 3 * index) % 16, 0)
        both = jnp.concatenate([main, blank], axis=0)
        return jnp.where(in_north, north, jnp.where(in_south, south, both))

    for start in range(0, wide, CHUNK):
        part = slice(start, start + CHUNK)
        from_pair, from_cross = pair[:, part], cross[:, part]
        for index in range(5):
            hyd[index, :, part] = circle(own[index, :, part], index, from_pair, from_cross)
    for start in range(0, cols, CHUNK):
        part = slice(start, start + CHUNK)
        middle = pair[:, wide + 2 * cols + start : wide + 2 * cols + start + CHUNK]
        outer = cross[:, wide + start : wide + start + CHUNK]
        beyond = jnp.where(
            left, above[FIELDS : FIELDS + 16, part], below[2 * FIELDS : 2 * FIELDS + 16, part]
        )
        replaced = (left & in_north) | (jnp.logical_not(left) & in_south)
        for index in range(5):
            field = tile[index, :, part]
            swapped = jnp.concatenate([field[8:16], field[0:8]], axis=0)
            here = jnp.where(left, field, swapped)
            far = jnp.where(
                left,
                pltpu.roll(beyond, (13 - 3 * index) % 16, 0),
                pltpu.roll(beyond, (8 - 3 * index) % 16, 0),
            )
            here = jnp.where(replaced, far, here)
            if index < 4:
                place = wide + (index // 2) * cols + start
                top = (index % 2) * 8
            else:
                place = wide + 3 * cols + start % half_cols
                top = 0 if start < half_cols else 8
            there = circle(pair[top : top + 8, place : place + CHUNK], index, middle, outer)
            base[index, :, part] = jnp.where(left, here, there)
            base[index, :, cols + start : cols + start + CHUNK] = jnp.where(left, there, here)

    def neighbours(ref, start):
        stop = start + CHUNK
        zero = jnp.zeros((16, LANES), F32)
        here = ref[:, start:stop]
        right = ref[:, stop : stop + LANES] if stop < wide else zero
        leftward = ref[:, start - LANES : start] if start else zero
        return here, east_of(here, right), west_of(here, leftward), pltpu.roll(here, 15, 0), pltpu.roll(here, 1, 0)

    for start in range(0, wide, CHUNK):
        part = slice(start, start + CHUNK)
        here, east, west, south, north = neighbours(base.at[0], start)
        drag = base[3, :, part]
        diagonal = relax(jnp.where(here > 0.0, 1.0, 0.0)) + drag
        for comp, (col_factor, row_factor) in enumerate(FACTORS):
            mid, mid_e, mid_w, mid_s, mid_n = neighbours(base.at[1 + comp], start)
            low[comp, :, part] = mid
            low[2 + comp, :, part] = diagonal * mid + here * (
                col_factor * (east * (mid - mid_e) + west * (mid - mid_w))
                + row_factor * (south * (mid - mid_s) + north * (mid - mid_n))
            )
        low[4, :, part] = drag
        low[5, :, part] = base[4, :, part]
        prev, prev_e, prev_w, prev_s, prev_n = neighbours(hyd.at[0], start)
        burden, sheet = hyd[1, :, part], hyd[2, :, part]
        to_east, _, to_west, _, _ = neighbours(hyd.at[3], start)
        to_south = hyd[4, :, part]
        to_north = pltpu.roll(to_south, 1, 0)
        total = storage + (to_east + to_west + to_south + to_north)
        creep = sheet * jnp.abs(burden - prev)
        known = storage * prev + creep * burden
        known += to_east * prev_e + to_west * prev_w + to_south * prev_s + to_north * prev_n
        for index, value in enumerate(
            (storage * prev, burden, sheet, to_east, to_west, to_south, to_north, total, known, total + creep)
        ):
            plan[index, :, part] = value


def weights_kernel(gathered, weights):
    first, second = krylov_weights(gathered[...])
    weights[0] = jnp.broadcast_to(first, (8, LANES))
    weights[1] = jnp.broadcast_to(second, (8, LANES))


def hydrology_kernel(info, weights, low, plan, potential, sheet_next, keep, give, now, then, fixed, opens):
    first, second = weights[0, 0:1, 0:1], weights[1, 0:1, 0:1]
    left = info[0] == 0
    wide = low.shape[2]
    cols = wide // 2
    row = row_index(16, CHUNK)
    outside = ((info[1] == 1) & (row >= 13)) | ((info[2] == 1) & (row >= 8) & (row <= 10))
    for start in range(0, wide, CHUNK):
        part = slice(start, start + CHUNK)
        one = first * low[0, :, part] + second * low[2, :, part]
        two = first * low[1, :, part] + second * low[3, :, part]
        slide_sq = one * one + two * two
        lifted = slide_sq + speed_floor
        speed = lifted * lax.rsqrt(lifted)
        melt = melt_factor * (low[5, :, part] + low[4, :, part] * slide_sq)
        opening = speed * jnp.maximum(bump_height - plan[2, :, part], 0.0)
        opens[:, part] = opening[0:8]
        gain = melt - opening
        fixed[:, part] = plan[0, :, part] + gain
        now[:, part] = jnp.where(outside, 0.0, (plan[8, :, part] + gain) / plan[9, :, part])

    def relaxed(ref, start):
        part = slice(start, start + CHUNK)
        stop = start + CHUNK
        zero = jnp.zeros((16, LANES), F32)
        here = ref[:, part]
        east = east_of(here, ref[:, stop : stop + LANES] if stop < wide else zero)
        west = west_of(here, ref[:, start - LANES : start] if start else zero)
        burden = plan[1, :, part]
        creep = plan[2, :, part] * jnp.abs(burden - here)
        top = fixed[:, part] + creep * burden
        top += plan[3, :, part] * east + plan[4, :, part] * west
        top += plan[5, :, part] * pltpu.roll(here, 15, 0) + plan[6, :, part] * pltpu.roll(here, 1, 0)
        return top / (plan[7, :, part] + creep)

    here, there = now, then
    for _ in range(HYD_ITERS - 2):
        for start in range(0, wide, CHUNK):
            there[:, start : start + CHUNK] = jnp.where(outside, 0.0, relaxed(here, start))
        here, there = there, here
    for start in range(0, cols, CHUNK):
        sides = []
        for begin in (start, cols + start):
            part = slice(begin, begin + CHUNK)
            value = relaxed(here, begin)[0:8]
            sheet = plan[2, 0:8, part]
            pressure = plan[1, 0:8, part] - value
            potential[:, part] = value
            sheet_next[:, part] = sheet + time_step * (
                opens[:, part] - sheet * jnp.abs(pressure) * pressure
            )
            sides.append(pressure)
        part = slice(start, start + CHUNK)
        keep[:, part] = jnp.where(left, sides[0], sides[1])
        give[:, part] = jnp.where(left, sides[1], sides[0])


def velocity_kernel(weights, force, image, out, staged, done):
    layers = image.shape[1]
    first, second = weights[0, 0:1, 0:1], weights[1, 0:1, 0:1]

    def copy(layer):
        return pltpu.make_async_copy(staged.at[:, layer], out.at[:, layer], done.at[layer])

    def step(layer, carry):
        for comp in range(2):
            staged[comp, layer] = first * force[comp] + second * image[comp, layer]
        copy(layer).start()
        return carry

    lax.fori_loop(0, layers, step, 0)

    def finish(layer, carry):
        copy(layer).wait()
        return carry

    lax.fori_loop(0, layers, finish, 0)


def call(kernel, out_shape, n_in, scratch=(), smem=(), far=(), out_space=pltpu.VMEM, **kwargs):
    outs = out_shape if isinstance(out_shape, (list, tuple)) else (out_shape,)
    specs = tuple(whole(out_space) for _ in outs)
    return pl.pallas_call(
        kernel,
        out_shape=out_shape,
        in_specs=[
            whole(pltpu.SMEM if i in smem else pltpu.HBM if i in far else pltpu.VMEM) for i in range(n_in)
        ],
        out_specs=specs if isinstance(out_shape, (list, tuple)) else specs[0],
        scratch_shapes=list(scratch),
        compiler_params=pltpu.CompilerParams(vmem_limit_bytes=22 << 20),
        **kwargs,
    )


def moved(value, axis, steps):
    count = lax.axis_size(axis)
    leading, last = (max(0, -steps), min(count, count - steps))
    return lax.ppermute(value, axis, [(source, source + steps) for source in range(leading, last)])


def body(
    viscosity,
    driving_stress,
    ice_mask,
    float_mask,
    friction,
    geothermal,
    potential_prev,
    overburden,
    sheet_thick,
    channel_east,
    channel_south,
    channel_area,
):
    layers, rows, cols = viscosity.shape
    side, band = lax.axis_index("hyd"), lax.axis_index("ice")
    bands = lax.axis_size("ice")
    info = jnp.stack([side, (side == 0) & (band == 0), (side == 1) & (band == bands - 1)]).astype(jnp.int32)
    swap = [(0, 1), (1, 0)]
    fixed_inputs = (
        potential_prev,
        overburden,
        sheet_thick,
        channel_east,
        channel_south,
        channel_area,
        viscosity,
        driving_stress,
        ice_mask,
        float_mask,
        friction,
        geothermal,
    )
    placed_inputs = tuple(pltpu.with_memory_space_constraint(array, pltpu.HBM) for array in fixed_inputs)
    raw = placed_inputs[6:11]
    types = (jnp.bfloat16, F32, jnp.int32, jnp.int32, F32)

    def buffers(last):
        return [pltpu.VMEM(array.shape[:-1] + (last,), kind) for array, kind in zip(raw, types)]

    message = call(
        edge_kernel,
        shape_of(rows, LANES),
        6,
        scratch=buffers(LANES) + [pltpu.SemaphoreType.DMA((5,))],
        smem=(0,),
        far=range(1, 6),
    )(info, *raw)
    message, late = lax.optimization_barrier((message, info))
    received = lax.ppermute(message, "hyd", swap)
    strip_rows, full = potential_prev.shape
    own, tile, pair, cross = call(
        strip_kernel,
        [
            shape_of(5, strip_rows, full),
            shape_of(5, rows, cols),
            shape_of(rows, full + 3 * cols + cols // 2),
            shape_of(rows, full + cols),
        ],
        13,
        scratch=[
            pltpu.VMEM(array.shape[1:] if slot == 6 else array.shape, array.dtype)
            for slot, array in enumerate(fixed_inputs)
        ]
        + [pltpu.SemaphoreType.DMA((12,))],
        smem=(0,),
        far=range(1, 13),
    )(late, *placed_inputs)
    pair_in = lax.ppermute(pair, "hyd", swap)
    roots, lines, force, fric, cover, fringe = call(
        root_kernel,
        [shape_of(layers, rows, cols), shape_of(3, FIELDS, cols), shape_of(2, rows, cols), shape_of(rows, cols), shape_of(rows, cols), shape_of(2, rows, cols)],
        6,
        scratch=buffers(cols) + [pltpu.VMEM((rows, cols), F32), pltpu.SemaphoreType.DMA((cols // FETCH, 6))],
        far=range(6),
    )(*placed_inputs[6:])
    wide = cols + LANES
    block, to_south, to_north = call(
        unpack_kernel,
        [shape_of(FIELDS, rows, LANES), shape_of(FIELDS + 16, wide), shape_of(2 * FIELDS + 16, wide)],
        4,
        smem=(0,),
    )(info, received, lines, fringe)
    above = moved(to_south, "ice", 1)
    below = moved(to_north, "ice", -1)
    strip_rows, full = potential_prev.shape
    meet = [(2 * index + 1, 2 * index + 2) for index in range(bands - 1)]
    cross_in = lax.ppermute(cross, AXES, meet + [(high, low) for low, high in meet])
    count = lax.axis_size("ice") * lax.axis_size("hyd")
    started, to_east, faces = call(
        image_kernel,
        [shape_of(2, layers, rows, cols), shape_of(layers, rows, cols), shape_of(layers, rows, cols)],
        5,
        scratch=[pltpu.VMEM((8, rows, cols), F32), pltpu.VMEM((2, 2, rows, cols), F32)],
    )(roots, force, fric, cover, block)
    image, faces, sums = call(
        moment_kernel,
        [shape_of(2, layers, rows, cols), shape_of(layers, rows, cols), shape_of(count, 1, LANES)],
        11,
        scratch=[
            pltpu.VMEM((2, FIELDS, cols), F32),
            pltpu.VMEM((2, rows, LANES), F32),
            pltpu.VMEM((4, FIELDS, cols), F32),
            pltpu.VMEM((FIELDS, cols), F32),
            pltpu.VMEM((3, rows, cols), F32),
        ],
        input_output_aliases={8: 0, 10: 1},
    )(roots, force, fric, cover, block, above, below, lines, started, to_east, faces)
    gathered = lax.all_to_all(sums, AXES, 0, 0, tiled=True)
    weights = call(weights_kernel, shape_of(2, 8, LANES), 1)(gathered)
    low, plan = call(
        assemble_kernel,
        [shape_of(6, rows, full), shape_of(10, rows, full)],
        7,
        scratch=[pltpu.VMEM((5, rows, full), F32), pltpu.VMEM((5, rows, full), F32)],
        smem=(0,),
    )(info, own, tile, pair_in, cross_in, above, below)
    potential, sheet_next, keep, give = call(
        hydrology_kernel,
        [
            shape_of(strip_rows, full),
            shape_of(strip_rows, full),
            shape_of(strip_rows, cols),
            shape_of(strip_rows, cols),
        ],
        4,
        scratch=[pltpu.VMEM((rows, full), F32)] * 3 + [pltpu.VMEM((strip_rows, full), F32)],
        smem=(0,),
    )(info, weights, low, plan)
    got = lax.ppermute(give, "hyd", swap)
    velocity = pl.pallas_call(
        velocity_kernel,
        out_shape=shape_of(2, layers, rows, cols),
        in_specs=[whole(), whole(), whole()],
        out_specs=whole(pltpu.HBM),
        scratch_shapes=[pltpu.VMEM((2, layers, rows, cols), F32), pltpu.SemaphoreType.DMA((layers,))],
        compiler_params=pltpu.CompilerParams(vmem_limit_bytes=22 << 20),
    )(weights, force, pltpu.with_memory_space_constraint(image, pltpu.VMEM))

    is_left = side == 0
    effective = jnp.concatenate([jnp.where(is_left, keep, got), jnp.where(is_left, got, keep)], axis=0)
    return (velocity, effective, potential, sheet_next)


def solution(mesh):
    tiles = P("ice", "hyd")
    layered = P(None, "ice", "hyd")
    strips = P(("ice", "hyd"), None)

    return jax.shard_map(
        body,
        mesh=mesh,
        in_specs=(layered, layered, tiles, tiles, tiles, tiles) + (strips,) * 6,
        out_specs=(P(None, None, "ice", "hyd"), tiles, strips, strips),
        check_vma=False,
    )
```

```python
import jax
import jax.numpy as jnp
from jax import lax
from jax.experimental import pallas as pl
from jax.experimental.pallas import tpu as pltpu
from jax.sharding import PartitionSpec as P


HYD_ITERS = 3
relax_weight = 0.1
melt_factor = 0.5
sheet_conduct = 2.0
channel_conduct = 1.5
storage = 1.0
bump_height = 0.3
time_step = 0.5
speed_floor = 0.25

AXES = ("ice", "hyd")
F32 = jnp.float32
LANES = 128
CHUNK = 512
FETCH = 1536
FACTORS = ((4.0, 1.0), (1.0, 4.0))
FIELDS = 24
F0, FG, MASK = 20, 22, 23


def whole(space=pltpu.VMEM):
    return pl.BlockSpec(memory_space=space)


def shape_of(*dims):
    return jax.ShapeDtypeStruct(dims, F32)


def lane_index(rows, cols):
    return lax.broadcasted_iota(jnp.int32, (rows, cols), 1)


def row_index(rows, cols):
    return lax.broadcasted_iota(jnp.int32, (rows, cols), 0)


def east_of(value, right):
    cols = value.shape[1]
    joined = jnp.concatenate([value, right], axis=1)
    return pltpu.roll(joined, cols + LANES - 1, 1)[:, :cols]


def west_of(value, left):
    joined = jnp.concatenate([left, value], axis=1)
    return pltpu.roll(joined, 1, 1)[:, LANES:]


LOW, HIGH = 2.0**9, 2.0**20
SPLIT = 2.0**11
TO_SOUTH, TO_NORTH = 24, 32


def packed_pair(upper, lower):
    return upper * HIGH + lower * LOW


def unpacked_pair(value):
    upper = jnp.floor(value * (1.0 / SPLIT))
    lower = value - upper * SPLIT
    return safe_root(upper * (1.0 / LOW)), safe_root(lower * (1.0 / LOW))


def safe_root(weight):
    present = weight > 0.0
    return jnp.where(present, root(jnp.where(present, weight, 1.0)), 0.0)


def root(weight):
    weight = weight.astype(F32)
    return weight * lax.rsqrt(weight)


def edge_kernel(half, visc, drive, mask, floating, friction, message, w, d, m, fl, fr, done):
    layers, rows, cols = visc.shape
    left_half = half[0] == 0
    start = pl.multiple_of(jnp.where(left_half, cols - LANES, 0), LANES)
    cut = pl.ds(start, LANES)
    copies = [
        pltpu.make_async_copy(source.at[..., cut], target, done.at[index])
        for index, (source, target) in enumerate(
            ((visc, w), (drive, d), (mask, m), (floating, fl), (friction, fr))
        )
    ]
    for copy in copies:
        copy.start()
    for copy in copies:
        copy.wait()
    first = jnp.where(left_half, LANES - 2, 0)
    lane = lane_index(rows, LANES)
    keep = (lane >= first) & (lane < first + 2)
    cover = m[...].astype(F32)
    fields = [w[layer].astype(F32) * cover for layer in range(layers)]
    fields += [d[comp] * cover for comp in range(2)]
    fields += [fr[...] * (cover * (1.0 - fl[...].astype(F32))), cover]
    total = jnp.zeros((rows, LANES), F32)
    for index, field in enumerate(fields):
        part = jnp.where(keep, field, 0.0)
        total += pltpu.roll(part, 2 * index, 1) if index else part
    message[...] = total


def root_kernel(
    visc,
    drive,
    mask,
    floating,
    friction,
    geothermal,
    roots,
    lines,
    force,
    fric,
    covers,
    to_south,
    to_north,
    w,
    d,
    m,
    fl,
    fr,
    geo,
    done,
):
    layers, rows, cols = visc.shape
    starts = list(range(0, cols, FETCH))

    def copies(index):
        part = slice(starts[index], starts[index] + FETCH)
        return [
            pltpu.make_async_copy(source.at[..., part], target.at[..., part], done.at[index, slot])
            for slot, (source, target) in enumerate(
                ((visc, w), (drive, d), (mask, m), (floating, fl), (friction, fr), (geothermal, geo))
            )
        ]

    for index in range(len(starts)):
        for copy in copies(index):
            copy.start()
    for index, begin in enumerate(starts):
        for copy in copies(index):
            copy.wait()
        for start in range(begin, begin + FETCH, CHUNK):
            part = slice(start, start + CHUNK)
            cover = m[:, part].astype(F32)
            grounded = cover * (1.0 - fl[:, part].astype(F32))
            drag = fr[:, part] * grounded
            fric[:, part] = drag
            covers[:, part] = cover
            pushes = [d[comp, :, part] * cover for comp in range(2)]
            for comp in range(2):
                force[comp, :, part] = pushes[comp]

            depth = layers // 2

            def step(layer, carry, part=part, cover=cover, depth=depth):
                pair = [w[index, :, part].astype(F32) for index in (layer, layer + depth)]
                for weight, index in zip(pair, (layer, layer + depth)):
                    value = root(weight) * cover
                    roots[index, :, part] = value
                    for slot, row in enumerate((0, rows - 1)):
                        lines[slot, pl.ds(index, 1), part] = value[row : row + 1]
                upper, lower = (weight * cover for weight in pair)

                def packed(row):
                    return packed_pair(upper[row : row + 1], lower[row : row + 1])

                to_south[pl.ds(layer, 1), part] = packed(rows - 1)
                to_north[pl.ds(layer, 1), part] = packed(0)
                to_north[pl.ds(layer + depth + 4, 1), part] = packed(1)
                return carry

            lax.fori_loop(0, depth, step, 0, unroll=5)
            lowest = roots[0, :, part]
            given = [lowest, pushes[0], pushes[1], drag, geo[:, part]]
            for slot, row in enumerate((0, rows - 1)):
                for comp in range(2):
                    lines[slot, F0 + comp : F0 + comp + 1, part] = pushes[comp][row : row + 1]

            def send(target, place, fields, row, part=part):
                for index, field in enumerate(fields):
                    target[place + index : place + index + 1, part] = field[row : row + 1]

            send(to_south, 10, given[1:], rows - 1)
            send(to_south, 14, given, rows - 2)
            send(to_south, 19, given[:3], rows - 3)
            send(to_north, 10, given[1:], 0)
            send(to_north, 24, given[1:], 1)
            send(to_north, 28, given[:3], 2)
            nothing = jnp.zeros((1, CHUNK), F32)
            to_south[22:23, part] = nothing
            to_south[23:24, part] = nothing
            to_north[31:32, part] = nothing


def unpack_kernel(half, message, south_rows_own, north_rows_own, block, to_south, to_north):
    rows = message.shape[0]
    cols = south_rows_own.shape[1]
    first = jnp.where(half[0] == 0, 0, LANES - 2)
    lane = lane_index(rows, LANES)
    keep = (lane >= first) & (lane < first + 2)
    packed = message[...]
    to_south[:, :cols] = south_rows_own[...]
    to_north[:, :cols] = north_rows_own[...]
    to_south[:, cols:] = jnp.zeros((TO_SOUTH, LANES), F32)
    to_north[:, cols:] = jnp.zeros((TO_NORTH, LANES), F32)
    parts = []
    for index in range(FIELDS):
        part = pltpu.roll(packed, LANES - 2 * index, 1) if index else packed
        parts.append(jnp.where(keep, part, 0.0))
        block[index] = safe_root(parts[index]) if index < F0 else parts[index]
    depth = F0 // 2
    for index in range(depth):
        pair = packed_pair(parts[index], parts[index + depth])
        to_south[index : index + 1, cols:] = pair[rows - 1 : rows]
        to_north[index : index + 1, cols:] = pair[0:1]
        to_north[depth + 4 + index : depth + 5 + index, cols:] = pair[1:2]
    for comp in range(2):
        push = parts[F0 + comp]
        to_south[10 + comp : 11 + comp, cols:] = push[rows - 1 : rows]
        to_north[10 + comp : 11 + comp, cols:] = push[0:1]
        to_north[24 + comp : 25 + comp, cols:] = push[1:2]


def line_of(ref, layer, start, size):
    if size > LANES:
        return ref[pl.ds(layer, 1), start : start + size]
    return ref[pl.ds(layer, 1), start - LANES : start + size][:, LANES:]


def fold(value):
    total = None
    for row in range(0, value.shape[0], 8):
        for col in range(0, value.shape[1], LANES):
            part = value[row : row + 8, col : col + LANES]
            total = part if total is None else total + part
    return total


def relax(cover):
    return (1.0 - cover) + relax_weight * cover


def south_rows(value, below):
    upper, lower = value[0:8], value[8:16]
    last = row_index(8, value.shape[1]) == 7
    next_row = pltpu.roll(lower, 7, 0)
    return jnp.concatenate(
        [jnp.where(last, next_row, pltpu.roll(upper, 7, 0)), jnp.where(last, below, next_row)], axis=0
    )


def north_rows(value, above):
    upper, lower = value[0:8], value[8:16]
    first = row_index(8, value.shape[1]) == 0
    previous = pltpu.roll(upper, 1, 0)
    return jnp.concatenate(
        [jnp.where(first, above, previous), jnp.where(first, previous, pltpu.roll(lower, 1, 0))], axis=0
    )


def columns(read_own, read_block, start, size, cols, rows):
    if start == cols:
        return read_block(), read_own(slice(cols - LANES, cols)), jnp.zeros((rows, LANES), F32)
    left = read_own(slice(start - LANES, start)) if start else read_block()
    stop = start + size
    right = read_own(slice(stop, stop + LANES)) if stop < cols else read_block()
    return read_own(slice(start, stop)), left, right


def image_kernel(roots, force, fric, mask, block, image, to_east, to_south, slopes, scaled):
    layers, rows, cols = roots.shape
    chunks = [(start, CHUNK) for start in range(0, cols, CHUNK)]
    for start, size in chunks:
        part = slice(start, start + size)
        nothing = jnp.zeros((1, size), F32)
        plain = relax(mask[:, part])
        for comp, (col_factor, row_factor) in enumerate(FACTORS):
            here, left, right = columns(
                lambda cut, comp=comp: force[comp, :, cut],
                lambda comp=comp: block[F0 + comp],
                start,
                size,
                cols,
                rows,
            )
            slopes[4 * comp, :, part] = col_factor * (here - east_of(here, right))
            slopes[4 * comp + 1, :, part] = col_factor * (here - west_of(here, left))
            slopes[4 * comp + 2, :, part] = row_factor * (here - south_rows(here, nothing))
            slopes[4 * comp + 3, :, part] = row_factor * (here - north_rows(here, nothing))
            scaled[0, comp, :, part] = plain * here
            scaled[1, comp, :, part] = (plain + fric[:, part]) * here

    def layer_step(layer, carry):
        kind = jnp.where(layer == 0, 1, 0)
        for start, size in chunks:
            part = slice(start, start + size)
            nothing = jnp.zeros((1, size), F32)
            here, left, right = columns(
                lambda cut: roots[layer, :, cut], lambda: block[layer], start, size, cols, rows
            )
            east = here * east_of(here, right)
            west = here * west_of(here, left)
            south = here * south_rows(here, nothing)
            north = north_rows(south, nothing)
            to_east[layer, :, part] = east
            to_south[layer, :, part] = south
            for comp in range(2):
                image[comp, layer, :, part] = scaled[kind, comp, :, part] + (
                    east * slopes[4 * comp, :, part]
                    + west * slopes[4 * comp + 1, :, part]
                    + south * slopes[4 * comp + 2, :, part]
                    + north * slopes[4 * comp + 3, :, part]
                )
        return carry

    lax.fori_loop(0, layers, layer_step, 0)


def moment_kernel(
    roots,
    force,
    fric,
    mask,
    block,
    above,
    below,
    lines,
    started,
    to_east,
    faces_before,
    image,
    faces,
    sums,
    line,
    edge,
    repair,
    outer,
    totals,
    over,
    under,
    beyond,
):
    layers, rows, cols = roots.shape
    chunks = [(start, CHUNK) for start in range(0, cols, CHUNK)]
    block_part = slice(cols, cols + LANES)

    depth = layers // 2
    for start, size in chunks + [(cols, LANES)]:
        part = slice(start, start + size)
        for source, place, target in ((above, 0, over), (below, 0, under), (below, depth + 4, beyond)):
            target[0:depth, part], target[depth:layers, part] = unpacked_pair(
                source[place : place + depth, part]
            )

    for start, size in chunks:
        part = slice(start, start + size)
        stop = start + size
        before = slice(start - LANES, start) if start else block_part
        after = slice(stop, stop + LANES)
        here = under[0:layers, part]
        top = lines[0, 0:layers, part] * over[0:layers, part]
        north = here * lines[1, 0:layers, part]
        outer[0:layers, part] = north
        east = here * east_of(here, under[0:layers, after])
        west = here * west_of(here, under[0:layers, before])
        south = here * beyond[0:layers, part]
        drag = jnp.where(row_index(layers, size) == 0, below[12:13, part], 0.0)
        full = relax(jnp.where(here[0:1] > 0.0, 1.0, 0.0)) + drag
        for comp, (col_factor, row_factor) in enumerate(FACTORS):
            row = slice(F0 + comp, F0 + comp + 1)
            sent = slice(10 + comp, 11 + comp)
            mid = below[sent, part]
            rise = row_factor * (mid - lines[1, row, part])
            repair[comp, 0:layers, part] = top * (row_factor * (lines[0, row, part] - above[sent, part]))
            repair[2 + comp, 0:layers, part] = north * (-rise)
            line[comp, 0:layers, part] = full * mid + (
                col_factor
                * (
                    east * (mid - east_of(mid, below[sent, after]))
                    + west * (mid - west_of(mid, below[sent, before]))
                )
                + (row_factor * south * (mid - below[24 + comp : 25 + comp, part]) + north * rise)
            )
        for index in range(3):
            totals[index, :, part] = jnp.zeros((rows, size), F32)

    nothing = jnp.zeros((rows, LANES), F32)
    side_slopes = []
    for comp, (col_factor, row_factor) in enumerate(FACTORS):
        here = block[F0 + comp]
        left = force[comp, :, cols - LANES : cols]
        up = above[10 + comp : 11 + comp, block_part]
        down = below[10 + comp : 11 + comp, block_part]
        side_slopes.append(
            (
                col_factor * (here - east_of(here, nothing)),
                col_factor * (here - west_of(here, left)),
                row_factor * (here - south_rows(here, down)),
                row_factor * (here - north_rows(here, up)),
            )
        )
    side_plain = relax(block[MASK])

    def layer_step(layer, carry):
        lower = jnp.maximum(layer - 1, 0)
        here = block[layer]
        east = here * east_of(here, nothing)
        west = here * west_of(here, roots[layer, :, cols - LANES : cols])
        south = here * south_rows(here, line_of(under, layer, cols, LANES))
        north = here * north_rows(here, line_of(over, layer, cols, LANES))
        full = side_plain + jnp.where(layer == 0, 1.0, 0.0) * block[FG]
        for comp in range(2):
            slope = side_slopes[comp]
            edge[comp] = full * block[F0 + comp] + (
                (east * slope[0] + west * slope[1]) + (south * slope[2] + north * slope[3])
            )
        for start, size in chunks:
            part = slice(start, start + size)
            faces[layer, rows - 1 : rows, part] = outer[pl.ds(layer, 1), part]
            for comp in range(2):
                image[comp, layer, 0:1, part] = (
                    image[comp, layer, 0:1, part] + repair[comp, pl.ds(layer, 1), part]
                )
                image[comp, layer, rows - 1 : rows, part] = (
                    image[comp, layer, rows - 1 : rows, part] + repair[2 + comp, pl.ds(layer, 1), part]
                )
        quads, singles = carry
        for start, size in chunks:
            part = slice(start, start + size)
            stop = start + size
            east = to_east[layer, :, part]
            south = faces[layer, :, part]
            down = roots[layer, :, part] * roots[lower, :, part]
            squares, falls = [], []
            lows, length = None, None
            for comp in range(2):
                value = image[comp, layer, :, part]
                right = image[comp, layer, :, stop : stop + LANES] if stop < cols else edge[comp]
                step = value - east_of(value, right)
                squares.append(step * step)
                step = value - south_rows(value, line[comp, pl.ds(layer, 1), part])
                falls.append(step * step)
                step = value - image[comp, lower, :, part]
                lows = step * step if lows is None else lows + step * step
                length = value * value if length is None else length + value * value
                totals[comp, :, part] += value
            totals[2, :, part] += length
            quads += fold(east * squares[0] + south * falls[1] + down * lows)
            singles += fold(east * squares[1] + south * falls[0])
        return quads, singles

    zero = jnp.zeros((8, LANES), F32)
    quads, singles = lax.fori_loop(0, layers, layer_step, (zero, zero))
    norm, cross, square, energy = zero, zero, zero, 4.0 * quads + singles
    for start, size in chunks:
        part = slice(start, start + size)
        one, two = force[0, :, part], force[1, :, part]
        norm += fold(one * one + two * two)
        cross += fold(one * totals[0, :, part] + two * totals[1, :, part])
        length = totals[2, :, part]
        square += fold(length)
        one, two = image[0, 0, :, part], image[1, 0, :, part]
        energy += fold(relax(mask[:, part]) * length + fric[:, part] * (one * one + two * two))
    lane = lane_index(1, LANES)
    packed = jnp.zeros((1, LANES), F32)
    for index, part in enumerate((layers * norm, cross, square, energy)):
        packed = jnp.where(lane == index, jnp.sum(part), packed)
    sums[...] = jnp.broadcast_to(packed[None], sums.shape)


def krylov_weights(gathered):
    total = jnp.sum(gathered, axis=0)
    lane = lane_index(1, LANES)

    def moment(index):
        return jnp.sum(jnp.where(lane == index, total, 0.0), axis=1, keepdims=True)

    norm, cross, square, energy = (moment(index) for index in range(4))
    step_one = norm / cross
    norm_next = step_one * (step_one * square - 2.0 * cross) + norm
    lead = 1.0 + norm_next / norm
    curve = lead * lead * cross - 2.0 * lead * step_one * square + step_one * step_one * energy
    sound = (norm_next > 0.0) & (curve > 0.0)
    step_two = jnp.where(sound, norm_next / jnp.where(sound, curve, 1.0), 0.0)
    return step_one + step_two * lead, -step_two * step_one


def placed(value, source_row, target_row):
    rows, cols = value.shape
    moved_rows = pltpu.roll(value, (rows - source_row) % rows, 0) if source_row % rows else value
    kept = jnp.where(row_index(rows, cols) < 3, moved_rows, 0.0)
    return pltpu.roll(kept, target_row % rows, 0) if target_row % rows else kept


def strip_kernel(info, *refs):
    sources, outs = refs[:12], refs[12:16]
    own, tile, pair, cross = outs
    buffers, done = refs[16:28], refs[28]
    copies = [
        pltpu.make_async_copy(source.at[0] if slot == 6 else source, target, done.at[slot])
        for slot, (source, target) in enumerate(zip(sources, buffers))
    ]
    for copy in copies:
        copy.start()
    for copy in copies[:6]:
        copy.wait()
    prev, burden, sheet, chan_east, chan_south, area, w, d, m, fl, fr, geo = buffers
    left = info[0] == 0
    wide = prev.shape[1]
    cols = w.shape[1]
    half_cols = cols // 2
    for start in range(0, wide, CHUNK):
        part = slice(start, start + CHUNK)
        base = sheet_conduct * sheet[:, part]
        fields = [
            prev[:, part],
            burden[:, part],
            sheet[:, part],
            base + channel_conduct * chan_east[:, part].astype(F32) * area[:, part],
            base + channel_conduct * chan_south[:, part].astype(F32) * area[:, part],
        ]
        first, last = None, None
        for index, field in enumerate(fields):
            own[index, :, part] = field
            both = jnp.concatenate([field, field], axis=0)
            head, tail = placed(both, 0, 3 * index), placed(both, 5, 3 * index)
            first = head if first is None else first + head
            last = tail if last is None else last + tail
        pair[:, part] = jnp.where(left, last, first)
        cross[:, part] = jnp.where(left, first, last)
    for copy in copies[6:]:
        copy.wait()
    for start in range(0, cols, CHUNK):
        part = slice(start, start + CHUNK)

        def shifted_part(offset, start=start):
            return slice(wide + offset + start, wide + offset + start + CHUNK)

        cover = m[:, part].astype(F32)
        fields = [
            root(w[:, part]) * cover,
            d[0, :, part] * cover,
            d[1, :, part] * cover,
            fr[:, part] * (cover * (1.0 - fl[:, part].astype(F32))),
            geo[:, part],
        ]
        first, last, middle, halves = None, None, None, []
        for index, field in enumerate(fields):
            tile[index, :, part] = field
            head, tail = placed(field, 0, 3 * index), placed(field, 13, 3 * index)
            inner = jnp.where(left, placed(field, 5, 3 * index), placed(field, 8, 3 * index))
            first = head if first is None else first + head
            last = tail if last is None else last + tail
            middle = inner if middle is None else middle + inner
            halves.append(jnp.where(left, field[8:16], field[0:8]))
        cross[:, shifted_part(0)] = jnp.where(left, first, last)
        pair[:, shifted_part(0)] = jnp.concatenate(halves[0:2], axis=0)
        pair[:, shifted_part(cols)] = jnp.concatenate(halves[2:4], axis=0)
        pair[:, shifted_part(2 * cols)] = middle
        row = 0 if start < half_cols else 8
        place = wide + 3 * cols + start % half_cols
        pair[row : row + 8, place : place + CHUNK] = halves[4]


def assemble_kernel(info, own, tile, pair, cross, above, below, low, plan, base, hyd):
    left = info[0] == 0
    wide = own.shape[2]
    cols = tile.shape[2]
    half_cols = cols // 2
    row = row_index(16, CHUNK)
    in_north = row >= 13
    in_south = (row >= 8) & (row <= 10)
    blank = jnp.zeros((8, CHUNK), F32)

    def circle(main, index, mine, theirs):
        north = jnp.where(left, theirs, mine)
        south = jnp.where(left, mine, theirs)
        north = pltpu.roll(north, (13 - 3 * index) % 16, 0)
        south = pltpu.roll(south, (8 - 3 * index) % 16, 0)
        both = jnp.concatenate([main, blank], axis=0)
        return jnp.where(in_north, north, jnp.where(in_south, south, both))

    for start in range(0, wide, CHUNK):
        part = slice(start, start + CHUNK)
        from_pair, from_cross = pair[:, part], cross[:, part]
        for index in range(5):
            hyd[index, :, part] = circle(own[index, :, part], index, from_pair, from_cross)
    for start in range(0, cols, CHUNK):
        part = slice(start, start + CHUNK)
        middle = pair[:, wide + 2 * cols + start : wide + 2 * cols + start + CHUNK]
        outer = cross[:, wide + start : wide + start + CHUNK]
        first_north, _ = unpacked_pair(above[0:1, part])
        first_south, _ = unpacked_pair(below[0:1, part])
        second_south, _ = unpacked_pair(below[14:15, part])
        nothing = jnp.zeros((1, CHUNK), F32)
        replaced = (left & in_north) | (jnp.logical_not(left) & in_south)
        for index in range(5):
            field = tile[index, :, part]
            swapped = jnp.concatenate([field[8:16], field[0:8]], axis=0)
            here = jnp.where(left, field, swapped)
            if index == 0:
                ups = above[19:20, part], above[14:15, part], first_north
                downs = first_south, second_south, below[28:29, part]
            else:
                near, next_near, next_far = 9 + index, 14 + index, 23 + index
                last = index < 3
                ups = (
                    above[19 + index : 20 + index, part] if last else nothing,
                    above[next_near : next_near + 1, part],
                    above[near : near + 1, part],
                )
                downs = (
                    below[near : near + 1, part],
                    below[next_far : next_far + 1, part],
                    below[28 + index : 29 + index, part] if last else nothing,
                )
            north = jnp.where(row == 13, ups[0], jnp.where(row == 14, ups[1], ups[2]))
            south = jnp.where(row == 8, downs[0], jnp.where(row == 9, downs[1], downs[2]))
            far = jnp.where(left, north, south)
            here = jnp.where(replaced, far, here)
            if index < 4:
                place = wide + (index // 2) * cols + start
                top = (index % 2) * 8
            else:
                place = wide + 3 * cols + start % half_cols
                top = 0 if start < half_cols else 8
            there = circle(pair[top : top + 8, place : place + CHUNK], index, middle, outer)
            base[index, :, part] = jnp.where(left, here, there)
            base[index, :, cols + start : cols + start + CHUNK] = jnp.where(left, there, here)

    def neighbours(ref, start):
        stop = start + CHUNK
        zero = jnp.zeros((16, LANES), F32)
        here = ref[:, start:stop]
        right = ref[:, stop : stop + LANES] if stop < wide else zero
        leftward = ref[:, start - LANES : start] if start else zero
        return here, east_of(here, right), west_of(here, leftward), pltpu.roll(here, 15, 0), pltpu.roll(here, 1, 0)

    for start in range(0, wide, CHUNK):
        part = slice(start, start + CHUNK)
        here, east, west, south, north = neighbours(base.at[0], start)
        drag = base[3, :, part]
        diagonal = relax(jnp.where(here > 0.0, 1.0, 0.0)) + drag
        for comp, (col_factor, row_factor) in enumerate(FACTORS):
            mid, mid_e, mid_w, mid_s, mid_n = neighbours(base.at[1 + comp], start)
            low[comp, :, part] = mid
            low[2 + comp, :, part] = diagonal * mid + here * (
                col_factor * (east * (mid - mid_e) + west * (mid - mid_w))
                + row_factor * (south * (mid - mid_s) + north * (mid - mid_n))
            )
        low[4, :, part] = drag
        low[5, :, part] = base[4, :, part]
        prev, prev_e, prev_w, prev_s, prev_n = neighbours(hyd.at[0], start)
        burden, sheet = hyd[1, :, part], hyd[2, :, part]
        to_east, _, to_west, _, _ = neighbours(hyd.at[3], start)
        to_south = hyd[4, :, part]
        to_north = pltpu.roll(to_south, 1, 0)
        total = storage + (to_east + to_west + to_south + to_north)
        creep = sheet * jnp.abs(burden - prev)
        known = storage * prev + creep * burden
        known += to_east * prev_e + to_west * prev_w + to_south * prev_s + to_north * prev_n
        for index, value in enumerate(
            (storage * prev, burden, sheet, to_east, to_west, to_south, to_north, total, known, total + creep)
        ):
            plan[index, :, part] = value


def weights_kernel(gathered, weights):
    first, second = krylov_weights(gathered[...])
    weights[0] = jnp.broadcast_to(first, (8, LANES))
    weights[1] = jnp.broadcast_to(second, (8, LANES))


def hydrology_kernel(info, weights, low, plan, potential, sheet_next, keep, give, now, then, fixed, opens):
    first, second = weights[0, 0:1, 0:1], weights[1, 0:1, 0:1]
    left = info[0] == 0
    wide = low.shape[2]
    cols = wide // 2
    row = row_index(16, CHUNK)
    outside = ((info[1] == 1) & (row >= 13)) | ((info[2] == 1) & (row >= 8) & (row <= 10))
    for start in range(0, wide, CHUNK):
        part = slice(start, start + CHUNK)
        one = first * low[0, :, part] + second * low[2, :, part]
        two = first * low[1, :, part] + second * low[3, :, part]
        slide_sq = one * one + two * two
        lifted = slide_sq + speed_floor
        speed = lifted * lax.rsqrt(lifted)
        melt = melt_factor * (low[5, :, part] + low[4, :, part] * slide_sq)
        opening = speed * jnp.maximum(bump_height - plan[2, :, part], 0.0)
        opens[:, part] = opening[0:8]
        gain = melt - opening
        fixed[:, part] = plan[0, :, part] + gain
        now[:, part] = jnp.where(outside, 0.0, (plan[8, :, part] + gain) / plan[9, :, part])

    def relaxed(ref, start):
        part = slice(start, start + CHUNK)
        stop = start + CHUNK
        zero = jnp.zeros((16, LANES), F32)
        here = ref[:, part]
        east = east_of(here, ref[:, stop : stop + LANES] if stop < wide else zero)
        west = west_of(here, ref[:, start - LANES : start] if start else zero)
        burden = plan[1, :, part]
        creep = plan[2, :, part] * jnp.abs(burden - here)
        top = fixed[:, part] + creep * burden
        top += plan[3, :, part] * east + plan[4, :, part] * west
        top += plan[5, :, part] * pltpu.roll(here, 15, 0) + plan[6, :, part] * pltpu.roll(here, 1, 0)
        return top / (plan[7, :, part] + creep)

    here, there = now, then
    for _ in range(HYD_ITERS - 2):
        for start in range(0, wide, CHUNK):
            there[:, start : start + CHUNK] = jnp.where(outside, 0.0, relaxed(here, start))
        here, there = there, here
    for start in range(0, cols, CHUNK):
        sides = []
        for begin in (start, cols + start):
            part = slice(begin, begin + CHUNK)
            value = relaxed(here, begin)[0:8]
            sheet = plan[2, 0:8, part]
            pressure = plan[1, 0:8, part] - value
            potential[:, part] = value
            sheet_next[:, part] = sheet + time_step * (
                opens[:, part] - sheet * jnp.abs(pressure) * pressure
            )
            sides.append(pressure)
        part = slice(start, start + CHUNK)
        keep[:, part] = jnp.where(left, sides[0], sides[1])
        give[:, part] = jnp.where(left, sides[1], sides[0])


def velocity_kernel(weights, force, image, out, staged, done):
    layers = image.shape[1]
    first, second = weights[0, 0:1, 0:1], weights[1, 0:1, 0:1]

    def copy(layer):
        return pltpu.make_async_copy(staged.at[:, layer], out.at[:, layer], done.at[layer])

    def step(layer, carry):
        for comp in range(2):
            staged[comp, layer] = first * force[comp] + second * image[comp, layer]
        copy(layer).start()
        return carry

    lax.fori_loop(0, layers, step, 0)

    def finish(layer, carry):
        copy(layer).wait()
        return carry

    lax.fori_loop(0, layers, finish, 0)


def call(kernel, out_shape, n_in, scratch=(), smem=(), far=(), out_space=pltpu.VMEM, **kwargs):
    outs = out_shape if isinstance(out_shape, (list, tuple)) else (out_shape,)
    specs = tuple(whole(out_space) for _ in outs)
    return pl.pallas_call(
        kernel,
        out_shape=out_shape,
        in_specs=[
            whole(pltpu.SMEM if i in smem else pltpu.HBM if i in far else pltpu.VMEM) for i in range(n_in)
        ],
        out_specs=specs if isinstance(out_shape, (list, tuple)) else specs[0],
        scratch_shapes=list(scratch),
        compiler_params=pltpu.CompilerParams(vmem_limit_bytes=22 << 20),
        **kwargs,
    )


def moved(value, axis, steps):
    count = lax.axis_size(axis)
    leading, last = (max(0, -steps), min(count, count - steps))
    return lax.ppermute(value, axis, [(source, source + steps) for source in range(leading, last)])


def body(
    viscosity,
    driving_stress,
    ice_mask,
    float_mask,
    friction,
    geothermal,
    potential_prev,
    overburden,
    sheet_thick,
    channel_east,
    channel_south,
    channel_area,
):
    layers, rows, cols = viscosity.shape
    side, band = lax.axis_index("hyd"), lax.axis_index("ice")
    bands = lax.axis_size("ice")
    info = jnp.stack([side, (side == 0) & (band == 0), (side == 1) & (band == bands - 1)]).astype(jnp.int32)
    swap = [(0, 1), (1, 0)]
    fixed_inputs = (
        potential_prev,
        overburden,
        sheet_thick,
        channel_east,
        channel_south,
        channel_area,
        viscosity,
        driving_stress,
        ice_mask,
        float_mask,
        friction,
        geothermal,
    )
    placed_inputs = tuple(pltpu.with_memory_space_constraint(array, pltpu.HBM) for array in fixed_inputs)
    raw = placed_inputs[6:11]
    types = (jnp.bfloat16, F32, jnp.int32, jnp.int32, F32)

    def buffers(last):
        return [pltpu.VMEM(array.shape[:-1] + (last,), kind) for array, kind in zip(raw, types)]

    message = call(
        edge_kernel,
        shape_of(rows, LANES),
        6,
        scratch=buffers(LANES) + [pltpu.SemaphoreType.DMA((5,))],
        smem=(0,),
        far=range(1, 6),
    )(info, *raw)
    message, late = lax.optimization_barrier((message, info))
    received = lax.ppermute(message, "hyd", swap)
    strip_rows, full = potential_prev.shape
    own, tile, pair, cross = call(
        strip_kernel,
        [
            shape_of(5, strip_rows, full),
            shape_of(5, rows, cols),
            shape_of(rows, full + 3 * cols + cols // 2),
            shape_of(rows, full + cols),
        ],
        13,
        scratch=[
            pltpu.VMEM(array.shape[1:] if slot == 6 else array.shape, array.dtype)
            for slot, array in enumerate(fixed_inputs)
        ]
        + [pltpu.SemaphoreType.DMA((12,))],
        smem=(0,),
        far=range(1, 13),
    )(late, *placed_inputs)
    pair_in = lax.ppermute(pair, "hyd", swap)
    roots, lines, force, fric, cover, south_own, north_own = call(
        root_kernel,
        [
            shape_of(layers, rows, cols),
            shape_of(2, FIELDS, cols),
            shape_of(2, rows, cols),
            shape_of(rows, cols),
            shape_of(rows, cols),
            shape_of(TO_SOUTH, cols),
            shape_of(TO_NORTH, cols),
        ],
        6,
        scratch=buffers(cols) + [pltpu.VMEM((rows, cols), F32), pltpu.SemaphoreType.DMA((cols // FETCH, 6))],
        far=range(6),
    )(*placed_inputs[6:])
    wide = cols + LANES
    block, to_south, to_north = call(
        unpack_kernel,
        [shape_of(FIELDS, rows, LANES), shape_of(TO_SOUTH, wide), shape_of(TO_NORTH, wide)],
        4,
        smem=(0,),
    )(info, received, south_own, north_own)
    above = moved(to_south, "ice", 1)
    below = moved(to_north, "ice", -1)
    strip_rows, full = potential_prev.shape
    meet = [(2 * index + 1, 2 * index + 2) for index in range(bands - 1)]
    cross_in = lax.ppermute(cross, AXES, meet + [(high, low) for low, high in meet])
    count = lax.axis_size("ice") * lax.axis_size("hyd")
    started, to_east, faces = call(
        image_kernel,
        [shape_of(2, layers, rows, cols), shape_of(layers, rows, cols), shape_of(layers, rows, cols)],
        5,
        scratch=[pltpu.VMEM((8, rows, cols), F32), pltpu.VMEM((2, 2, rows, cols), F32)],
    )(roots, force, fric, cover, block)
    image, faces, sums = call(
        moment_kernel,
        [shape_of(2, layers, rows, cols), shape_of(layers, rows, cols), shape_of(count, 1, LANES)],
        11,
        scratch=[
            pltpu.VMEM((2, FIELDS, cols), F32),
            pltpu.VMEM((2, rows, LANES), F32),
            pltpu.VMEM((4, FIELDS, cols), F32),
            pltpu.VMEM((FIELDS, cols), F32),
            pltpu.VMEM((3, rows, cols), F32),
        ]
        + [pltpu.VMEM((FIELDS, wide), F32)] * 3,
        input_output_aliases={8: 0, 10: 1},
    )(roots, force, fric, cover, block, above, below, lines, started, to_east, faces)
    gathered = lax.all_to_all(sums, AXES, 0, 0, tiled=True)
    weights = call(weights_kernel, shape_of(2, 8, LANES), 1)(gathered)
    low, plan = call(
        assemble_kernel,
        [shape_of(6, rows, full), shape_of(10, rows, full)],
        7,
        scratch=[pltpu.VMEM((5, rows, full), F32), pltpu.VMEM((5, rows, full), F32)],
        smem=(0,),
    )(info, own, tile, pair_in, cross_in, above, below)
    potential, sheet_next, keep, give = call(
        hydrology_kernel,
        [
            shape_of(strip_rows, full),
            shape_of(strip_rows, full),
            shape_of(strip_rows, cols),
            shape_of(strip_rows, cols),
        ],
        4,
        scratch=[pltpu.VMEM((rows, full), F32)] * 3 + [pltpu.VMEM((strip_rows, full), F32)],
        smem=(0,),
    )(info, weights, low, plan)
    got = lax.ppermute(give, "hyd", swap)
    velocity = pl.pallas_call(
        velocity_kernel,
        out_shape=shape_of(2, layers, rows, cols),
        in_specs=[whole(), whole(), whole()],
        out_specs=whole(pltpu.HBM),
        scratch_shapes=[pltpu.VMEM((2, layers, rows, cols), F32), pltpu.SemaphoreType.DMA((layers,))],
        compiler_params=pltpu.CompilerParams(vmem_limit_bytes=22 << 20),
    )(weights, force, pltpu.with_memory_space_constraint(image, pltpu.VMEM))

    is_left = side == 0
    effective = jnp.concatenate([jnp.where(is_left, keep, got), jnp.where(is_left, got, keep)], axis=0)
    return (velocity, effective, potential, sheet_next)


def solution(mesh):
    tiles = P("ice", "hyd")
    layered = P(None, "ice", "hyd")
    strips = P(("ice", "hyd"), None)

    return jax.shard_map(
        body,
        mesh=mesh,
        in_specs=(layered, layered, tiles, tiles, tiles, tiles) + (strips,) * 6,
        out_specs=(P(None, None, "ice", "hyd"), tiles, strips, strips),
        check_vma=False,
    )
```

```python
import jax
import jax.numpy as jnp
from jax import lax
from jax.experimental import pallas as pl
from jax.experimental.pallas import tpu as pltpu
from jax.sharding import PartitionSpec as P


HYD_ITERS = 3
relax_weight = 0.1
melt_factor = 0.5
sheet_conduct = 2.0
channel_conduct = 1.5
storage = 1.0
bump_height = 0.3
time_step = 0.5
speed_floor = 0.25

AXES = ("ice", "hyd")
F32 = jnp.float32
LANES = 128
CHUNK = 512
FETCH = 1536
FACTORS = ((4.0, 1.0), (1.0, 4.0))
FIELDS = 24
F0, FG, MASK = 20, 22, 23


def whole(space=pltpu.VMEM):
    return pl.BlockSpec(memory_space=space)


def shape_of(*dims):
    return jax.ShapeDtypeStruct(dims, F32)


def lane_index(rows, cols):
    return lax.broadcasted_iota(jnp.int32, (rows, cols), 1)


def row_index(rows, cols):
    return lax.broadcasted_iota(jnp.int32, (rows, cols), 0)


def east_of(value, right):
    cols = value.shape[1]
    joined = jnp.concatenate([value, right], axis=1)
    return pltpu.roll(joined, cols + LANES - 1, 1)[:, :cols]


def west_of(value, left):
    joined = jnp.concatenate([left, value], axis=1)
    return pltpu.roll(joined, 1, 1)[:, LANES:]


LOW, HIGH = 2.0**9, 2.0**20
SPLIT = 2.0**11
TO_SOUTH, TO_NORTH = 24, 32


def packed_pair(upper, lower):
    return upper * HIGH + lower * LOW


def unpacked_pair(value):
    upper = jnp.floor(value * (1.0 / SPLIT))
    lower = value - upper * SPLIT
    return safe_root(upper * (1.0 / LOW)), safe_root(lower * (1.0 / LOW))


def safe_root(weight):
    present = weight > 0.0
    return jnp.where(present, root(jnp.where(present, weight, 1.0)), 0.0)


def root(weight):
    weight = weight.astype(F32)
    return weight * lax.rsqrt(weight)


def edge_kernel(half, visc, drive, mask, floating, friction, message, w, d, m, fl, fr, done):
    layers, rows, cols = visc.shape
    left_half = half[0] == 0
    start = pl.multiple_of(jnp.where(left_half, cols - LANES, 0), LANES)
    cut = pl.ds(start, LANES)
    copies = [
        pltpu.make_async_copy(source.at[..., cut], target, done.at[index])
        for index, (source, target) in enumerate(
            ((visc, w), (drive, d), (mask, m), (floating, fl), (friction, fr))
        )
    ]
    for copy in copies:
        copy.start()
    for copy in copies:
        copy.wait()
    first = jnp.where(left_half, LANES - 2, 0)
    lane = lane_index(rows, LANES)
    keep = (lane >= first) & (lane < first + 2)
    cover = m[...].astype(F32)
    fields = [w[layer].astype(F32) * cover for layer in range(layers)]
    fields += [d[comp] * cover for comp in range(2)]
    fields += [fr[...] * (cover * (1.0 - fl[...].astype(F32))), cover]
    total = jnp.zeros((rows, LANES), F32)
    for index, field in enumerate(fields):
        part = jnp.where(keep, field, 0.0)
        total += pltpu.roll(part, 2 * index, 1) if index else part
    message[...] = total


def root_kernel(
    visc,
    drive,
    mask,
    floating,
    friction,
    geothermal,
    roots,
    lines,
    force,
    fric,
    covers,
    to_south,
    to_north,
    w,
    d,
    m,
    fl,
    fr,
    geo,
    done,
):
    layers, rows, cols = visc.shape
    starts = list(range(0, cols, FETCH))

    def copies(index):
        part = slice(starts[index], starts[index] + FETCH)
        return [
            pltpu.make_async_copy(source.at[..., part], target.at[..., part], done.at[index, slot])
            for slot, (source, target) in enumerate(
                ((visc, w), (drive, d), (mask, m), (floating, fl), (friction, fr), (geothermal, geo))
            )
        ]

    for index in range(len(starts)):
        for copy in copies(index):
            copy.start()
    for index, begin in enumerate(starts):
        for copy in copies(index):
            copy.wait()
        for start in range(begin, begin + FETCH, CHUNK):
            part = slice(start, start + CHUNK)
            cover = m[:, part].astype(F32)
            grounded = cover * (1.0 - fl[:, part].astype(F32))
            drag = fr[:, part] * grounded
            fric[:, part] = drag
            covers[:, part] = cover
            pushes = [d[comp, :, part] * cover for comp in range(2)]
            for comp in range(2):
                force[comp, :, part] = pushes[comp]

            depth = layers // 2

            def step(layer, carry, part=part, cover=cover, depth=depth):
                pair = [w[index, :, part].astype(F32) for index in (layer, layer + depth)]
                for weight, index in zip(pair, (layer, layer + depth)):
                    value = root(weight) * cover
                    roots[index, :, part] = value
                    for slot, row in enumerate((0, rows - 1)):
                        lines[slot, pl.ds(index, 1), part] = value[row : row + 1]
                upper, lower = (weight * cover for weight in pair)

                def packed(row):
                    return packed_pair(upper[row : row + 1], lower[row : row + 1])

                to_south[pl.ds(layer, 1), part] = packed(rows - 1)
                to_north[pl.ds(layer, 1), part] = packed(0)
                to_north[pl.ds(layer + depth + 4, 1), part] = packed(1)
                return carry

            lax.fori_loop(0, depth, step, 0, unroll=5)
            lowest = roots[0, :, part]
            given = [lowest, pushes[0], pushes[1], drag, geo[:, part]]
            for slot, row in enumerate((0, rows - 1)):
                for comp in range(2):
                    lines[slot, F0 + comp : F0 + comp + 1, part] = pushes[comp][row : row + 1]

            def send(target, place, fields, row, part=part):
                for index, field in enumerate(fields):
                    target[place + index : place + index + 1, part] = field[row : row + 1]

            send(to_south, 10, given[1:], rows - 1)
            send(to_south, 14, given, rows - 2)
            send(to_south, 19, given[:3], rows - 3)
            send(to_north, 10, given[1:], 0)
            send(to_north, 24, given[1:], 1)
            send(to_north, 28, given[:3], 2)
            nothing = jnp.zeros((1, CHUNK), F32)
            to_south[22:23, part] = nothing
            to_south[23:24, part] = nothing
            to_north[31:32, part] = nothing


def unpack_kernel(half, message, block, to_south, to_north):
    rows = message.shape[0]
    cols = to_south.shape[1] - LANES
    first = jnp.where(half[0] == 0, 0, LANES - 2)
    lane = lane_index(rows, LANES)
    keep = (lane >= first) & (lane < first + 2)
    packed = message[...]
    to_south[:, cols:] = jnp.zeros((TO_SOUTH, LANES), F32)
    to_north[:, cols:] = jnp.zeros((TO_NORTH, LANES), F32)
    parts = []
    for index in range(FIELDS):
        part = pltpu.roll(packed, LANES - 2 * index, 1) if index else packed
        parts.append(jnp.where(keep, part, 0.0))
        block[index] = safe_root(parts[index]) if index < F0 else parts[index]
    depth = F0 // 2
    for index in range(depth):
        pair = packed_pair(parts[index], parts[index + depth])
        to_south[index : index + 1, cols:] = pair[rows - 1 : rows]
        to_north[index : index + 1, cols:] = pair[0:1]
        to_north[depth + 4 + index : depth + 5 + index, cols:] = pair[1:2]
    for comp in range(2):
        push = parts[F0 + comp]
        to_south[10 + comp : 11 + comp, cols:] = push[rows - 1 : rows]
        to_north[10 + comp : 11 + comp, cols:] = push[0:1]
        to_north[24 + comp : 25 + comp, cols:] = push[1:2]


def opening_kernel(info, message, *refs):
    inputs, outs, rest = refs[:6], refs[6:13], refs[13:]
    roots, lines, force, fric, covers, to_south, to_north = outs[:7]
    block, scratch = rest[0], rest[1:]
    root_kernel(*inputs, roots, lines, force, fric, covers, to_south, to_north, *scratch)
    unpack_kernel(info, message, block, to_south, to_north)


def line_of(ref, layer, start, size):
    if size > LANES:
        return ref[pl.ds(layer, 1), start : start + size]
    return ref[pl.ds(layer, 1), start - LANES : start + size][:, LANES:]


def fold(value):
    total = None
    for row in range(0, value.shape[0], 8):
        for col in range(0, value.shape[1], LANES):
            part = value[row : row + 8, col : col + LANES]
            total = part if total is None else total + part
    return total


def relax(cover):
    return (1.0 - cover) + relax_weight * cover


def south_rows(value, below):
    upper, lower = value[0:8], value[8:16]
    last = row_index(8, value.shape[1]) == 7
    next_row = pltpu.roll(lower, 7, 0)
    return jnp.concatenate(
        [jnp.where(last, next_row, pltpu.roll(upper, 7, 0)), jnp.where(last, below, next_row)], axis=0
    )


def north_rows(value, above):
    upper, lower = value[0:8], value[8:16]
    first = row_index(8, value.shape[1]) == 0
    previous = pltpu.roll(upper, 1, 0)
    return jnp.concatenate(
        [jnp.where(first, above, previous), jnp.where(first, previous, pltpu.roll(lower, 1, 0))], axis=0
    )


def columns(read_own, read_block, start, size, cols, rows):
    if start == cols:
        return read_block(), read_own(slice(cols - LANES, cols)), jnp.zeros((rows, LANES), F32)
    left = read_own(slice(start - LANES, start)) if start else read_block()
    stop = start + size
    right = read_own(slice(stop, stop + LANES)) if stop < cols else read_block()
    return read_own(slice(start, stop)), left, right


def image_kernel(roots, force, fric, mask, block, image, to_east, to_south, slopes, scaled):
    layers, rows, cols = roots.shape
    chunks = [(start, CHUNK) for start in range(0, cols, CHUNK)]
    for start, size in chunks:
        part = slice(start, start + size)
        nothing = jnp.zeros((1, size), F32)
        plain = relax(mask[:, part])
        for comp, (col_factor, row_factor) in enumerate(FACTORS):
            here, left, right = columns(
                lambda cut, comp=comp: force[comp, :, cut],
                lambda comp=comp: block[F0 + comp],
                start,
                size,
                cols,
                rows,
            )
            slopes[4 * comp, :, part] = col_factor * (here - east_of(here, right))
            slopes[4 * comp + 1, :, part] = col_factor * (here - west_of(here, left))
            slopes[4 * comp + 2, :, part] = row_factor * (here - south_rows(here, nothing))
            slopes[4 * comp + 3, :, part] = row_factor * (here - north_rows(here, nothing))
            scaled[0, comp, :, part] = plain * here
            scaled[1, comp, :, part] = (plain + fric[:, part]) * here

    def layer_step(layer, carry):
        kind = jnp.where(layer == 0, 1, 0)
        for start, size in chunks:
            part = slice(start, start + size)
            nothing = jnp.zeros((1, size), F32)
            here, left, right = columns(
                lambda cut: roots[layer, :, cut], lambda: block[layer], start, size, cols, rows
            )
            east = here * east_of(here, right)
            west = here * west_of(here, left)
            south = here * south_rows(here, nothing)
            north = north_rows(south, nothing)
            to_east[layer, :, part] = east
            to_south[layer, :, part] = south
            for comp in range(2):
                image[comp, layer, :, part] = scaled[kind, comp, :, part] + (
                    east * slopes[4 * comp, :, part]
                    + west * slopes[4 * comp + 1, :, part]
                    + south * slopes[4 * comp + 2, :, part]
                    + north * slopes[4 * comp + 3, :, part]
                )
        return carry

    lax.fori_loop(0, layers, layer_step, 0, unroll=2)


def moment_kernel(
    roots,
    force,
    fric,
    mask,
    block,
    above,
    below,
    lines,
    started,
    to_east,
    faces_before,
    image,
    faces,
    sums,
    line,
    edge,
    repair,
    outer,
    totals,
    over,
    under,
    beyond,
):
    layers, rows, cols = roots.shape
    chunks = [(start, CHUNK) for start in range(0, cols, CHUNK)]
    block_part = slice(cols, cols + LANES)

    depth = layers // 2
    for start, size in chunks + [(cols, LANES)]:
        part = slice(start, start + size)
        for source, place, target in ((above, 0, over), (below, 0, under), (below, depth + 4, beyond)):
            target[0:depth, part], target[depth:layers, part] = unpacked_pair(
                source[place : place + depth, part]
            )

    for start, size in chunks:
        part = slice(start, start + size)
        stop = start + size
        before = slice(start - LANES, start) if start else block_part
        after = slice(stop, stop + LANES)
        here = under[0:layers, part]
        top = lines[0, 0:layers, part] * over[0:layers, part]
        north = here * lines[1, 0:layers, part]
        outer[0:layers, part] = north
        east = here * east_of(here, under[0:layers, after])
        west = here * west_of(here, under[0:layers, before])
        south = here * beyond[0:layers, part]
        drag = jnp.where(row_index(layers, size) == 0, below[12:13, part], 0.0)
        full = relax(jnp.where(here[0:1] > 0.0, 1.0, 0.0)) + drag
        for comp, (col_factor, row_factor) in enumerate(FACTORS):
            row = slice(F0 + comp, F0 + comp + 1)
            sent = slice(10 + comp, 11 + comp)
            mid = below[sent, part]
            rise = row_factor * (mid - lines[1, row, part])
            repair[comp, 0:layers, part] = top * (row_factor * (lines[0, row, part] - above[sent, part]))
            repair[2 + comp, 0:layers, part] = north * (-rise)
            line[comp, 0:layers, part] = full * mid + (
                col_factor
                * (
                    east * (mid - east_of(mid, below[sent, after]))
                    + west * (mid - west_of(mid, below[sent, before]))
                )
                + (row_factor * south * (mid - below[24 + comp : 25 + comp, part]) + north * rise)
            )
        for index in range(3):
            totals[index, :, part] = jnp.zeros((rows, size), F32)

    nothing = jnp.zeros((rows, LANES), F32)
    side_slopes = []
    for comp, (col_factor, row_factor) in enumerate(FACTORS):
        here = block[F0 + comp]
        left = force[comp, :, cols - LANES : cols]
        up = above[10 + comp : 11 + comp, block_part]
        down = below[10 + comp : 11 + comp, block_part]
        side_slopes.append(
            (
                col_factor * (here - east_of(here, nothing)),
                col_factor * (here - west_of(here, left)),
                row_factor * (here - south_rows(here, down)),
                row_factor * (here - north_rows(here, up)),
            )
        )
    side_plain = relax(block[MASK])

    def layer_step(layer, carry):
        lower = jnp.maximum(layer - 1, 0)
        here = block[layer]
        east = here * east_of(here, nothing)
        west = here * west_of(here, roots[layer, :, cols - LANES : cols])
        south = here * south_rows(here, line_of(under, layer, cols, LANES))
        north = here * north_rows(here, line_of(over, layer, cols, LANES))
        full = side_plain + jnp.where(layer == 0, 1.0, 0.0) * block[FG]
        for comp in range(2):
            slope = side_slopes[comp]
            edge[comp] = full * block[F0 + comp] + (
                (east * slope[0] + west * slope[1]) + (south * slope[2] + north * slope[3])
            )
        for start, size in chunks:
            part = slice(start, start + size)
            faces[layer, rows - 1 : rows, part] = outer[pl.ds(layer, 1), part]
            for comp in range(2):
                image[comp, layer, 0:1, part] = (
                    image[comp, layer, 0:1, part] + repair[comp, pl.ds(layer, 1), part]
                )
                image[comp, layer, rows - 1 : rows, part] = (
                    image[comp, layer, rows - 1 : rows, part] + repair[2 + comp, pl.ds(layer, 1), part]
                )
        quads, singles = carry
        for start, size in chunks:
            part = slice(start, start + size)
            stop = start + size
            east = to_east[layer, :, part]
            south = faces[layer, :, part]
            down = roots[layer, :, part] * roots[lower, :, part]
            squares, falls = [], []
            lows, length = None, None
            for comp in range(2):
                value = image[comp, layer, :, part]
                right = image[comp, layer, :, stop : stop + LANES] if stop < cols else edge[comp]
                step = value - east_of(value, right)
                squares.append(step * step)
                step = value - south_rows(value, line[comp, pl.ds(layer, 1), part])
                falls.append(step * step)
                step = value - image[comp, lower, :, part]
                lows = step * step if lows is None else lows + step * step
                length = value * value if length is None else length + value * value
                totals[comp, :, part] += value
            totals[2, :, part] += length
            quads += fold(east * squares[0] + south * falls[1] + down * lows)
            singles += fold(east * squares[1] + south * falls[0])
        return quads, singles

    zero = jnp.zeros((8, LANES), F32)
    quads, singles = lax.fori_loop(0, layers, layer_step, (zero, zero))
    norm, cross, square, energy = zero, zero, zero, 4.0 * quads + singles
    for start, size in chunks:
        part = slice(start, start + size)
        one, two = force[0, :, part], force[1, :, part]
        norm += fold(one * one + two * two)
        cross += fold(one * totals[0, :, part] + two * totals[1, :, part])
        length = totals[2, :, part]
        square += fold(length)
        one, two = image[0, 0, :, part], image[1, 0, :, part]
        energy += fold(relax(mask[:, part]) * length + fric[:, part] * (one * one + two * two))
    lane = lane_index(1, LANES)
    packed = jnp.zeros((1, LANES), F32)
    for index, part in enumerate((layers * norm, cross, square, energy)):
        packed = jnp.where(lane == index, jnp.sum(part), packed)
    sums[...] = jnp.broadcast_to(packed[None], sums.shape)


def krylov_weights(gathered):
    total = jnp.sum(gathered, axis=0)
    lane = lane_index(1, LANES)

    def moment(index):
        return jnp.sum(jnp.where(lane == index, total, 0.0), axis=1, keepdims=True)

    norm, cross, square, energy = (moment(index) for index in range(4))
    step_one = norm / cross
    norm_next = step_one * (step_one * square - 2.0 * cross) + norm
    lead = 1.0 + norm_next / norm
    curve = lead * lead * cross - 2.0 * lead * step_one * square + step_one * step_one * energy
    sound = (norm_next > 0.0) & (curve > 0.0)
    step_two = jnp.where(sound, norm_next / jnp.where(sound, curve, 1.0), 0.0)
    return step_one + step_two * lead, -step_two * step_one


def placed(value, source_row, target_row):
    rows, cols = value.shape
    moved_rows = pltpu.roll(value, (rows - source_row) % rows, 0) if source_row % rows else value
    kept = jnp.where(row_index(rows, cols) < 3, moved_rows, 0.0)
    return pltpu.roll(kept, target_row % rows, 0) if target_row % rows else kept


def strip_kernel(info, *refs):
    sources, outs = refs[:12], refs[12:16]
    own, tile, pair, cross = outs
    buffers, done = refs[16:28], refs[28]
    copies = [
        pltpu.make_async_copy(source.at[0] if slot == 6 else source, target, done.at[slot])
        for slot, (source, target) in enumerate(zip(sources, buffers))
    ]
    for copy in copies:
        copy.start()
    for copy in copies[:6]:
        copy.wait()
    prev, burden, sheet, chan_east, chan_south, area, w, d, m, fl, fr, geo = buffers
    left = info[0] == 0
    wide = prev.shape[1]
    cols = w.shape[1]
    half_cols = cols // 2
    for start in range(0, wide, CHUNK):
        part = slice(start, start + CHUNK)
        base = sheet_conduct * sheet[:, part]
        fields = [
            prev[:, part],
            burden[:, part],
            sheet[:, part],
            base + channel_conduct * chan_east[:, part].astype(F32) * area[:, part],
            base + channel_conduct * chan_south[:, part].astype(F32) * area[:, part],
        ]
        first, last = None, None
        for index, field in enumerate(fields):
            own[index, :, part] = field
            both = jnp.concatenate([field, field], axis=0)
            head, tail = placed(both, 0, 3 * index), placed(both, 5, 3 * index)
            first = head if first is None else first + head
            last = tail if last is None else last + tail
        pair[:, part] = jnp.where(left, last, first)
        cross[:, part] = jnp.where(left, first, last)
    for copy in copies[6:]:
        copy.wait()
    for start in range(0, cols, CHUNK):
        part = slice(start, start + CHUNK)

        def shifted_part(offset, start=start):
            return slice(wide + offset + start, wide + offset + start + CHUNK)

        cover = m[:, part].astype(F32)
        fields = [
            root(w[:, part]) * cover,
            d[0, :, part] * cover,
            d[1, :, part] * cover,
            fr[:, part] * (cover * (1.0 - fl[:, part].astype(F32))),
            geo[:, part],
        ]
        first, last, middle, halves = None, None, None, []
        for index, field in enumerate(fields):
            tile[index, :, part] = field
            head, tail = placed(field, 0, 3 * index), placed(field, 13, 3 * index)
            inner = jnp.where(left, placed(field, 5, 3 * index), placed(field, 8, 3 * index))
            first = head if first is None else first + head
            last = tail if last is None else last + tail
            middle = inner if middle is None else middle + inner
            halves.append(jnp.where(left, field[8:16], field[0:8]))
        cross[:, shifted_part(0)] = jnp.where(left, first, last)
        pair[:, shifted_part(0)] = jnp.concatenate(halves[0:2], axis=0)
        pair[:, shifted_part(cols)] = jnp.concatenate(halves[2:4], axis=0)
        pair[:, shifted_part(2 * cols)] = middle
        row = 0 if start < half_cols else 8
        place = wide + 3 * cols + start % half_cols
        pair[row : row + 8, place : place + CHUNK] = halves[4]


def assemble_kernel(info, own, tile, pair, cross, above, below, low, plan, base, hyd):
    left = info[0] == 0
    wide = own.shape[2]
    cols = tile.shape[2]
    half_cols = cols // 2
    row = row_index(16, CHUNK)
    in_north = row >= 13
    in_south = (row >= 8) & (row <= 10)
    blank = jnp.zeros((8, CHUNK), F32)

    def circle(main, index, mine, theirs):
        north = jnp.where(left, theirs, mine)
        south = jnp.where(left, mine, theirs)
        north = pltpu.roll(north, (13 - 3 * index) % 16, 0)
        south = pltpu.roll(south, (8 - 3 * index) % 16, 0)
        both = jnp.concatenate([main, blank], axis=0)
        return jnp.where(in_north, north, jnp.where(in_south, south, both))

    for start in range(0, wide, CHUNK):
        part = slice(start, start + CHUNK)
        from_pair, from_cross = pair[:, part], cross[:, part]
        for index in range(5):
            hyd[index, :, part] = circle(own[index, :, part], index, from_pair, from_cross)
    for start in range(0, cols, CHUNK):
        part = slice(start, start + CHUNK)
        middle = pair[:, wide + 2 * cols + start : wide + 2 * cols + start + CHUNK]
        outer = cross[:, wide + start : wide + start + CHUNK]
        first_north, _ = unpacked_pair(above[0:1, part])
        first_south, _ = unpacked_pair(below[0:1, part])
        second_south, _ = unpacked_pair(below[14:15, part])
        nothing = jnp.zeros((1, CHUNK), F32)
        replaced = (left & in_north) | (jnp.logical_not(left) & in_south)
        for index in range(5):
            field = tile[index, :, part]
            swapped = jnp.concatenate([field[8:16], field[0:8]], axis=0)
            here = jnp.where(left, field, swapped)
            if index == 0:
                ups = above[19:20, part], above[14:15, part], first_north
                downs = first_south, second_south, below[28:29, part]
            else:
                near, next_near, next_far = 9 + index, 14 + index, 23 + index
                last = index < 3
                ups = (
                    above[19 + index : 20 + index, part] if last else nothing,
                    above[next_near : next_near + 1, part],
                    above[near : near + 1, part],
                )
                downs = (
                    below[near : near + 1, part],
                    below[next_far : next_far + 1, part],
                    below[28 + index : 29 + index, part] if last else nothing,
                )
            north = jnp.where(row == 13, ups[0], jnp.where(row == 14, ups[1], ups[2]))
            south = jnp.where(row == 8, downs[0], jnp.where(row == 9, downs[1], downs[2]))
            far = jnp.where(left, north, south)
            here = jnp.where(replaced, far, here)
            if index < 4:
                place = wide + (index // 2) * cols + start
                top = (index % 2) * 8
            else:
                place = wide + 3 * cols + start % half_cols
                top = 0 if start < half_cols else 8
            there = circle(pair[top : top + 8, place : place + CHUNK], index, middle, outer)
            base[index, :, part] = jnp.where(left, here, there)
            base[index, :, cols + start : cols + start + CHUNK] = jnp.where(left, there, here)

    def neighbours(ref, start):
        stop = start + CHUNK
        zero = jnp.zeros((16, LANES), F32)
        here = ref[:, start:stop]
        right = ref[:, stop : stop + LANES] if stop < wide else zero
        leftward = ref[:, start - LANES : start] if start else zero
        return here, east_of(here, right), west_of(here, leftward), pltpu.roll(here, 15, 0), pltpu.roll(here, 1, 0)

    for start in range(0, wide, CHUNK):
        part = slice(start, start + CHUNK)
        here, east, west, south, north = neighbours(base.at[0], start)
        drag = base[3, :, part]
        diagonal = relax(jnp.where(here > 0.0, 1.0, 0.0)) + drag
        for comp, (col_factor, row_factor) in enumerate(FACTORS):
            mid, mid_e, mid_w, mid_s, mid_n = neighbours(base.at[1 + comp], start)
            low[comp, :, part] = mid
            low[2 + comp, :, part] = diagonal * mid + here * (
                col_factor * (east * (mid - mid_e) + west * (mid - mid_w))
                + row_factor * (south * (mid - mid_s) + north * (mid - mid_n))
            )
        low[4, :, part] = drag
        low[5, :, part] = base[4, :, part]
        prev, prev_e, prev_w, prev_s, prev_n = neighbours(hyd.at[0], start)
        burden, sheet = hyd[1, :, part], hyd[2, :, part]
        to_east, _, to_west, _, _ = neighbours(hyd.at[3], start)
        to_south = hyd[4, :, part]
        to_north = pltpu.roll(to_south, 1, 0)
        total = storage + (to_east + to_west + to_south + to_north)
        creep = sheet * jnp.abs(burden - prev)
        known = storage * prev + creep * burden
        known += to_east * prev_e + to_west * prev_w + to_south * prev_s + to_north * prev_n
        for index, value in enumerate(
            (storage * prev, burden, sheet, to_east, to_west, to_south, to_north, total, known, total + creep)
        ):
            plan[index, :, part] = value


def weights_kernel(gathered, weights):
    first, second = krylov_weights(gathered[...])
    weights[0] = jnp.broadcast_to(first, (8, LANES))
    weights[1] = jnp.broadcast_to(second, (8, LANES))


def hydrology_kernel(info, weights, low, plan, potential, sheet_next, keep, give, now, then, fixed, opens):
    first, second = weights[0, 0:1, 0:1], weights[1, 0:1, 0:1]
    left = info[0] == 0
    wide = low.shape[2]
    cols = wide // 2
    row = row_index(16, CHUNK)
    outside = ((info[1] == 1) & (row >= 13)) | ((info[2] == 1) & (row >= 8) & (row <= 10))
    for start in range(0, wide, CHUNK):
        part = slice(start, start + CHUNK)
        one = first * low[0, :, part] + second * low[2, :, part]
        two = first * low[1, :, part] + second * low[3, :, part]
        slide_sq = one * one + two * two
        lifted = slide_sq + speed_floor
        speed = lifted * lax.rsqrt(lifted)
        melt = melt_factor * (low[5, :, part] + low[4, :, part] * slide_sq)
        opening = speed * jnp.maximum(bump_height - plan[2, :, part], 0.0)
        opens[:, part] = opening[0:8]
        gain = melt - opening
        fixed[:, part] = plan[0, :, part] + gain
        now[:, part] = jnp.where(outside, 0.0, (plan[8, :, part] + gain) / plan[9, :, part])

    def relaxed(ref, start):
        part = slice(start, start + CHUNK)
        stop = start + CHUNK
        zero = jnp.zeros((16, LANES), F32)
        here = ref[:, part]
        east = east_of(here, ref[:, stop : stop + LANES] if stop < wide else zero)
        west = west_of(here, ref[:, start - LANES : start] if start else zero)
        burden = plan[1, :, part]
        creep = plan[2, :, part] * jnp.abs(burden - here)
        top = fixed[:, part] + creep * burden
        top += plan[3, :, part] * east + plan[4, :, part] * west
        top += plan[5, :, part] * pltpu.roll(here, 15, 0) + plan[6, :, part] * pltpu.roll(here, 1, 0)
        return top / (plan[7, :, part] + creep)

    here, there = now, then
    for _ in range(HYD_ITERS - 2):
        for start in range(0, wide, CHUNK):
            there[:, start : start + CHUNK] = jnp.where(outside, 0.0, relaxed(here, start))
        here, there = there, here
    for start in range(0, cols, CHUNK):
        sides = []
        for begin in (start, cols + start):
            part = slice(begin, begin + CHUNK)
            value = relaxed(here, begin)[0:8]
            sheet = plan[2, 0:8, part]
            pressure = plan[1, 0:8, part] - value
            potential[:, part] = value
            sheet_next[:, part] = sheet + time_step * (
                opens[:, part] - sheet * jnp.abs(pressure) * pressure
            )
            sides.append(pressure)
        part = slice(start, start + CHUNK)
        keep[:, part] = jnp.where(left, sides[0], sides[1])
        give[:, part] = jnp.where(left, sides[1], sides[0])


def closing_kernel(info, own, tile, pair, cross, above, below, weights, *refs):
    outs, (low, plan, base, hyd), rest = refs[:4], refs[4:8], refs[8:]
    assemble_kernel(info, own, tile, pair, cross, above, below, low, plan, base, hyd)
    hydrology_kernel(info, weights, low, plan, *outs, *rest)


def velocity_kernel(weights, force, image, out, staged, done):
    layers = image.shape[1]
    first, second = weights[0, 0:1, 0:1], weights[1, 0:1, 0:1]

    def copy(layer):
        return pltpu.make_async_copy(staged.at[:, layer], out.at[:, layer], done.at[layer])

    def step(layer, carry):
        for comp in range(2):
            staged[comp, layer] = first * force[comp] + second * image[comp, layer]
        copy(layer).start()
        return carry

    lax.fori_loop(0, layers, step, 0)

    def finish(layer, carry):
        copy(layer).wait()
        return carry

    lax.fori_loop(0, layers, finish, 0)


def call(kernel, out_shape, n_in, scratch=(), smem=(), far=(), out_space=pltpu.VMEM, **kwargs):
    outs = out_shape if isinstance(out_shape, (list, tuple)) else (out_shape,)
    specs = tuple(whole(out_space) for _ in outs)
    return pl.pallas_call(
        kernel,
        out_shape=out_shape,
        in_specs=[
            whole(pltpu.SMEM if i in smem else pltpu.HBM if i in far else pltpu.VMEM) for i in range(n_in)
        ],
        out_specs=specs if isinstance(out_shape, (list, tuple)) else specs[0],
        scratch_shapes=list(scratch),
        compiler_params=pltpu.CompilerParams(vmem_limit_bytes=22 << 20),
        **kwargs,
    )


def moved(value, axis, steps):
    count = lax.axis_size(axis)
    leading, last = (max(0, -steps), min(count, count - steps))
    return lax.ppermute(value, axis, [(source, source + steps) for source in range(leading, last)])


def body(
    viscosity,
    driving_stress,
    ice_mask,
    float_mask,
    friction,
    geothermal,
    potential_prev,
    overburden,
    sheet_thick,
    channel_east,
    channel_south,
    channel_area,
):
    layers, rows, cols = viscosity.shape
    side, band = lax.axis_index("hyd"), lax.axis_index("ice")
    bands = lax.axis_size("ice")
    info = jnp.stack([side, (side == 0) & (band == 0), (side == 1) & (band == bands - 1)]).astype(jnp.int32)
    swap = [(0, 1), (1, 0)]
    wide = cols + LANES
    fixed_inputs = (
        potential_prev,
        overburden,
        sheet_thick,
        channel_east,
        channel_south,
        channel_area,
        viscosity,
        driving_stress,
        ice_mask,
        float_mask,
        friction,
        geothermal,
    )
    placed_inputs = tuple(pltpu.with_memory_space_constraint(array, pltpu.HBM) for array in fixed_inputs)
    raw = placed_inputs[6:11]
    types = (jnp.bfloat16, F32, jnp.int32, jnp.int32, F32)

    def buffers(last):
        return [pltpu.VMEM(array.shape[:-1] + (last,), kind) for array, kind in zip(raw, types)]

    message = call(
        edge_kernel,
        shape_of(rows, LANES),
        6,
        scratch=buffers(LANES) + [pltpu.SemaphoreType.DMA((5,))],
        smem=(0,),
        far=range(1, 6),
    )(info, *raw)
    message, late = lax.optimization_barrier((message, info))
    received = lax.ppermute(message, "hyd", swap)
    strip_rows, full = potential_prev.shape
    own, tile, pair, cross = call(
        strip_kernel,
        [
            shape_of(5, strip_rows, full),
            shape_of(5, rows, cols),
            shape_of(rows, full + 3 * cols + cols // 2),
            shape_of(rows, full + cols),
        ],
        13,
        scratch=[
            pltpu.VMEM(array.shape[1:] if slot == 6 else array.shape, array.dtype)
            for slot, array in enumerate(fixed_inputs)
        ]
        + [pltpu.SemaphoreType.DMA((12,))],
        smem=(0,),
        far=range(1, 13),
    )(late, *placed_inputs)
    pair_in = lax.ppermute(pair, "hyd", swap)
    roots, lines, force, fric, cover, to_south, to_north, block = call(
        opening_kernel,
        [
            shape_of(layers, rows, cols),
            shape_of(2, FIELDS, cols),
            shape_of(2, rows, cols),
            shape_of(rows, cols),
            shape_of(rows, cols),
            shape_of(TO_SOUTH, wide),
            shape_of(TO_NORTH, wide),
            shape_of(FIELDS, rows, LANES),
        ],
        8,
        scratch=buffers(cols) + [pltpu.VMEM((rows, cols), F32), pltpu.SemaphoreType.DMA((cols // FETCH, 6))],
        smem=(0,),
        far=range(2, 8),
    )(info, received, *placed_inputs[6:])
    above = moved(to_south, "ice", 1)
    below = moved(to_north, "ice", -1)
    strip_rows, full = potential_prev.shape
    meet = [(2 * index + 1, 2 * index + 2) for index in range(bands - 1)]
    cross_in = lax.ppermute(cross, AXES, meet + [(high, low) for low, high in meet])
    count = lax.axis_size("ice") * lax.axis_size("hyd")
    started, to_east, faces = call(
        image_kernel,
        [shape_of(2, layers, rows, cols), shape_of(layers, rows, cols), shape_of(layers, rows, cols)],
        5,
        scratch=[pltpu.VMEM((8, rows, cols), F32), pltpu.VMEM((2, 2, rows, cols), F32)],
    )(roots, force, fric, cover, block)
    image, faces, sums = call(
        moment_kernel,
        [shape_of(2, layers, rows, cols), shape_of(layers, rows, cols), shape_of(count, 1, LANES)],
        11,
        scratch=[
            pltpu.VMEM((2, FIELDS, cols), F32),
            pltpu.VMEM((2, rows, LANES), F32),
            pltpu.VMEM((4, FIELDS, cols), F32),
            pltpu.VMEM((FIELDS, cols), F32),
            pltpu.VMEM((3, rows, cols), F32),
        ]
        + [pltpu.VMEM((FIELDS, wide), F32)] * 3,
        input_output_aliases={8: 0, 10: 1},
    )(roots, force, fric, cover, block, above, below, lines, started, to_east, faces)
    gathered = lax.all_to_all(sums, AXES, 0, 0, tiled=True)
    weights = call(weights_kernel, shape_of(2, 8, LANES), 1)(gathered)
    potential, sheet_next, keep, give = call(
        closing_kernel,
        [
            shape_of(strip_rows, full),
            shape_of(strip_rows, full),
            shape_of(strip_rows, cols),
            shape_of(strip_rows, cols),
        ],
        8,
        scratch=[pltpu.VMEM((count_of, rows, full), F32) for count_of in (6, 10, 5, 5)]
        + [pltpu.VMEM((rows, full), F32)] * 3
        + [pltpu.VMEM((strip_rows, full), F32)],
        smem=(0,),
    )(info, own, tile, pair_in, cross_in, above, below, weights)
    got = lax.ppermute(give, "hyd", swap)
    velocity = pl.pallas_call(
        velocity_kernel,
        out_shape=shape_of(2, layers, rows, cols),
        in_specs=[whole(), whole(), whole()],
        out_specs=whole(pltpu.HBM),
        scratch_shapes=[pltpu.VMEM((2, layers, rows, cols), F32), pltpu.SemaphoreType.DMA((layers,))],
        compiler_params=pltpu.CompilerParams(vmem_limit_bytes=22 << 20),
    )(weights, force, pltpu.with_memory_space_constraint(image, pltpu.VMEM))

    is_left = side == 0
    effective = jnp.concatenate([jnp.where(is_left, keep, got), jnp.where(is_left, got, keep)], axis=0)
    return (velocity, effective, potential, sheet_next)


def solution(mesh):
    tiles = P("ice", "hyd")
    layered = P(None, "ice", "hyd")
    strips = P(("ice", "hyd"), None)

    return jax.shard_map(
        body,
        mesh=mesh,
        in_specs=(layered, layered, tiles, tiles, tiles, tiles) + (strips,) * 6,
        out_specs=(P(None, None, "ice", "hyd"), tiles, strips, strips),
        check_vma=False,
    )
```
